32 devices in a mesh: dp: 8 (over y, x, core), tensor: 4 (over z).
Axes of the slice: x: 2, y: 2, z: 4, core: 2. Of those that a mesh axis runs over, the one named last changes fastest.
Arguments:
- latent_in: bfloat16 [16, 1024, 1408], P('dp', 'tensor'), may hold values from -6 to 6
- skip_in: bfloat16 [16, 1024, 1408], P('dp', 'tensor'), may hold values from -6 to 6
- text_emb: bfloat16 [16, 256, 1408], P('dp'), may hold values from -6 to 6
- text_length: int32 [16], P('dp'), may hold values from 64 to 256
- time_emb: bfloat16 [16, 1408], P('dp'), may hold values from -6 to 6
- grid_pos: int32 [16, 1024, 2], P('dp'), may hold values from 0 to 31
- skip_gain: bfloat16 [2816], replicated, may hold values from 0.5 to 1.5
- skip_beta: bfloat16 [2816], replicated, may hold values from -2 to 2
- skip_weight: bfloat16 [2816, 1408], P(None, 'tensor'), may hold values from -0.109375 to 0.109375
- skip_bias: bfloat16 [1408], P('tensor'), may hold values from -2 to 2
- ada_weight: bfloat16 [1408, 1408], P(None, 'tensor'), may hold values from -0.15625 to 0.15625
- ada_bias: bfloat16 [1408], P('tensor'), may hold values from -2 to 2
- query_key_value_weight: bfloat16 [3, 1408, 1408], P(None, None, 'tensor'), may hold values from -0.15625 to 0.15625
- qk_gain: bfloat16 [2, 88], replicated, may hold values from 0.5 to 1.5
- attention_output_weight: bfloat16 [1408, 1408], P('tensor'), may hold values from -3 to 3
- out_bias: bfloat16 [1408], replicated, may hold values from -2 to 2
- norm2_gain: bfloat16 [1408], replicated, may hold values from 0.5 to 1.5
- norm2_beta: bfloat16 [1408], replicated, may hold values from -2 to 2
- crossed_query_weight: bfloat16 [1408, 1408], P(None, 'tensor'), may hold values from -0.15625 to 0.15625
- cross_kv_weight: bfloat16 [2, 1408, 1408], P(None, None, 'tensor'), may hold values from -0.15625 to 0.15625
- cross_qk_gain: bfloat16 [2, 88], replicated, may hold values from 0.5 to 1.5
- crossed_output_weight: bfloat16 [1408, 1408], P('tensor'), may hold values from -1.5 to 1.5
- cross_out_bias: bfloat16 [1408], replicated, may hold values from -2 to 2
- norm3_gain: bfloat16 [1408], replicated, may hold values from 0.5 to 1.5
- norm3_beta: bfloat16 [1408], replicated, may hold values from -2 to 2
- up_projection_weight: bfloat16 [1408, 6144], P(None, 'tensor'), may hold values from -0.15625 to 0.15625
- up_bias: bfloat16 [6144], P('tensor'), may hold values from -2 to 2
- down_projection_weight: bfloat16 [6144, 1408], P('tensor'), may hold values from -0.078125 to 0.078125
- down_bias: bfloat16 [1408], replicated, may hold values from -2 to 2
- out_grad: bfloat16 [16, 1024, 1408], P('dp', 'tensor'), may hold values from -6 to 6
Outputs:
- output: bfloat16 [16, 1024, 1408], P('dp', 'tensor')
- stats: float32 [16, 5, 1024], P('dp', None, 'tensor')
- latent_grad: float32 [16, 1024, 1408], P('dp', 'tensor')
- skip_grad: float32 [16, 1024, 1408], P('dp', 'tensor')
- text_grad: float32 [16, 256, 1408], P('dp')
- time_grad: float32 [16, 1408], P('dp')
- skip_gain_grad: float32 [2816], replicated
- skip_beta_grad: float32 [2816], replicated
- skip_weight_grad: float32 [2816, 1408], P(None, 'tensor')
- skip_bias_grad: float32 [1408], P('tensor')
- ada_weight_grad: float32 [1408, 1408], P(None, 'tensor')
- ada_bias_grad: float32 [1408], P('tensor')
- qkv_weight_grad: float32 [3, 1408, 1408], P(None, None, 'tensor')
- qk_gain_grad: float32 [2, 88], replicated
- out_weight_grad: float32 [1408, 1408], P('tensor')
- out_bias_grad: float32 [1408], replicated
- norm2_gain_grad: float32 [1408], replicated
- norm2_beta_grad: float32 [1408], replicated
- cross_query_weight_grad: float32 [1408, 1408], P(None, 'tensor')
- cross_kv_weight_grad: float32 [2, 1408, 1408], P(None, None, 'tensor')
- cross_qk_gain_grad: float32 [2, 88], replicated
- cross_out_weight_grad: float32 [1408, 1408], P('tensor')
- cross_out_bias_grad: float32 [1408], replicated
- norm3_gain_grad: float32 [1408], replicated
- norm3_beta_grad: float32 [1408], replicated
- up_projection_gradient: float32 [1408, 6144], P(None, 'tensor')
- up_bias_grad: float32 [6144], P('tensor')
- down_weight_grad: float32 [6144, 1408], P('tensor')
- down_bias_grad: float32 [1408], replicated
The draws below stay inside these ranges and needn't reach their ends.
All inputs are finite; a program needn't handle non-finite values.
Results may differ from the reference program's by a relative error of at most 0.033.
Values may be sent and summed in bfloat16 or wider, within the bound.
No kernel may reach another device: no remote copies, remote signals or barrier semaphores. Data moves between devices by JAX's collectives and lax.ppermute only.
A program may use at most 320 MiB of HBM per device.

```python
import jax
import jax.numpy as jnp
from jax import lax

D = 1408
H = 16
HD = 88
FF = 6144
TXT = 256
GRID = 32
SEQ_DEV = 2
SEQ_LEN = 1024
SEQS = 16


def place_ends(drawn, stream_key, low, largest):
    longest = drawn.shape.index(max(drawn.shape))
    spots = []
    for shift in (0, 1):
        where = [jax.random.randint(jax.random.fold_in(stream_key, axis), (), 0, length) for axis, length in enumerate(drawn.shape)]
        where[longest] = (where[longest] + shift) % drawn.shape[longest]
        spots.append(tuple(where))
    return drawn.at[spots[0]].set(low).at[spots[1]].set(largest)


def block_scale(own_key, extent, pieces, least, high):
    loudness, own = 1.0, jax.random.fold_in(own_key, 6)
    for dim, parts in pieces:
        steps = jnp.exp(jax.random.uniform(jax.random.fold_in(own, dim), (parts,), jnp.float32, least / len(pieces), high / len(pieces)))
        loudness = loudness * jnp.repeat(steps, extent[dim] // parts).reshape([-1 if axis == dim else 1 for axis in range(len(extent))])
    return loudness


def scatter_about(own_key, shape, deviation, most, shards=(), held_as=jnp.bfloat16):
    drawn = jax.random.normal(own_key, shape, jnp.float32) * deviation
    if len(shards) > 0:
        drawn = block_scale(own_key, shape, shards, -0.22, 0.18) * drawn
    return jnp.clip(drawn, min=-most, max=most).astype(held_as)


def setup_inputs(seed: int = 0) -> dict:
    splits = jax.random.split(jax.random.key(seed), 31)
    return {
        "latent_in": scatter_about(splits[0], (SEQS, SEQ_LEN, D), 1.0, 6.0, ((0, 8), (1, 4))),
        "skip_in": scatter_about(splits[1], (SEQS, SEQ_LEN, D), 1.0, 6.0, ((0, 8), (1, 4))),
        "text_emb": scatter_about(splits[2], (SEQS, TXT, D), 1.0, 6.0, ((0, 8),)),
        "text_length": place_ends(jax.random.randint(splits[3], (SEQS,), TXT // 4, TXT + 1), jax.random.fold_in(splits[3], 1), TXT // 4, TXT).astype(jnp.int32),
        "time_emb": scatter_about(splits[4], (SEQS, D), 1.0, 6.0, ((0, 8),)),
        "grid_pos": place_ends(jax.random.randint(splits[5], (SEQS, SEQ_LEN, 2), 0, GRID), jax.random.fold_in(splits[5], 1), 0, GRID - 1).astype(jnp.int32),
        "skip_gain": jnp.clip(1.0 + 0.1 * jax.random.normal(splits[6], (2 * D,), jnp.float32), 0.5, 1.5).astype(jnp.bfloat16),
        "skip_beta": scatter_about(splits[7], (2 * D,), 0.3, 2.0),
        "skip_weight": scatter_about(splits[8], (2 * D, D), (2 * D) ** -0.5, 0.109375, ((1, 4),)),
        "skip_bias": scatter_about(splits[9], (D,), 0.3, 2.0, ((0, 4),)),
        "ada_weight": scatter_about(splits[10], (D, D), D ** -0.5, 0.15625, ((1, 4),)),
        "ada_bias": scatter_about(splits[11], (D,), 0.3, 2.0, ((0, 4),)),
        "query_key_value_weight": scatter_about(splits[12], (3, D, D), D ** -0.5, 0.15625, ((2, 4),)),
        "qk_gain": jnp.clip(1.0 + 0.1 * jax.random.normal(splits[13], (2, HD), jnp.float32), 0.5, 1.5).astype(jnp.bfloat16),
        "attention_output_weight": scatter_about(splits[14], (D, D), 4 ** -0.5, 3.0, ((0, 4),)),
        "out_bias": scatter_about(splits[15], (D,), 0.3, 2.0),
        "norm2_gain": jnp.clip(1.0 + 0.1 * jax.random.normal(splits[16], (D,), jnp.float32), 0.5, 1.5).astype(jnp.bfloat16),
        "norm2_beta": scatter_about(splits[17], (D,), 0.3, 2.0),
        "crossed_query_weight": scatter_about(splits[18], (D, D), D ** -0.5, 0.15625, ((1, 4),)),
        "cross_kv_weight": scatter_about(splits[19], (2, D, D), D ** -0.5, 0.15625, ((2, 4),)),
        "cross_qk_gain": jnp.clip(1.0 + 0.1 * jax.random.normal(splits[20], (2, HD), jnp.float32), 0.5, 1.5).astype(jnp.bfloat16),
        "crossed_output_weight": scatter_about(splits[21], (D, D), 16 ** -0.5, 1.5, ((0, 4),)),
        "cross_out_bias": scatter_about(splits[22], (D,), 0.3, 2.0),
        "norm3_gain": jnp.clip(1.0 + 0.1 * jax.random.normal(splits[23], (D,), jnp.float32), 0.5, 1.5).astype(jnp.bfloat16),
        "norm3_beta": scatter_about(splits[24], (D,), 0.3, 2.0),
        "up_projection_weight": scatter_about(splits[25], (D, FF), D ** -0.5, 0.15625, ((1, 4),)),
        "up_bias": scatter_about(splits[26], (FF,), 0.3, 2.0, ((0, 4),)),
        "down_projection_weight": scatter_about(splits[27], (FF, D), FF ** -0.5, 0.078125, ((0, 4),)),
        "down_bias": scatter_about(splits[28], (D,), 0.3, 2.0),
        "out_grad": scatter_about(splits[29], (SEQS, SEQ_LEN, D), 1.0, 6.0, ((0, 8), (1, 4))),
    }


EPSILON = 1e-06
ROPE_BASE = 10000.0
PRECISE = lax.Precision.HIGHEST

@jax.custom_vjp
def low(v):
    return lax.optimization_barrier(v.astype(jnp.bfloat16)).astype(jnp.float32)

@jax.custom_vjp
def low_back(v):
    return v

def low_keep(v):
    return (low(v), None)

def low_pass(kept, grad):
    return (grad,)

def back_keep(v):
    return (v, None)

def back_low(kept, grad):
    return (low(grad),)
low.defvjp(low_keep, low_pass)
low_back.defvjp(back_keep, back_low)

def layer_norm(values):
    center = values - lax.optimization_barrier(jnp.mean(values, -1, keepdims=True))
    return center * lax.rsqrt(lax.optimization_barrier(jnp.mean(center * center, -1, keepdims=True)) + EPSILON)

def rope_tables(grid_pos):
    quarter = HD // 4
    frequency = ROPE_BASE ** (-jnp.arange(quarter, dtype=jnp.float32) / quarter)
    row_angle = grid_pos[..., 0:1].astype(jnp.float32) * frequency
    col_angle = grid_pos[..., 1:2].astype(jnp.float32) * frequency
    angles = jnp.concatenate([row_angle, row_angle, col_angle, col_angle], -1)
    return (jnp.cos(angles)[..., None, :], jnp.sin(angles)[..., None, :])

def rotate(values, cosines, sine_table):
    quarter = HD // 4
    first = values[..., :quarter]
    second = values[..., quarter:2 * quarter]
    third = values[..., 2 * quarter:3 * quarter]
    fourth = values[..., 3 * quarter:]
    turned = jnp.concatenate([-second, first, -fourth, third], -1)
    return values * cosines + turned * sine_table

def matmul(left, right):
    return jnp.matmul(left, right, precision=PRECISE)

def attend(query_in, keys_in, values_in, key_bias):
    groups, length, head_count, head_size = query_in.shape
    block_rows = min(512, length)
    query_blocks = jnp.moveaxis(query_in.reshape(groups, length // block_rows, block_rows, head_count, head_size), 1, 0)

    def one_block(portion):
        scores = jnp.einsum('gqhd,gkhd->ghqk', portion, keys_in, precision=PRECISE) * HD ** (-0.5) + key_bias[:, None, None, :]
        scores = low_back(scores)
        weights = low(jax.nn.softmax(scores, -1))
        return jnp.einsum('ghqk,gkhd->gqhd', weights, values_in, precision=PRECISE)
    results = lax.map(jax.checkpoint(one_block), query_blocks)
    return jnp.moveaxis(results, 0, 1).reshape(groups, length, head_count * head_size)

def root_mean(values):
    return jnp.sqrt(lax.optimization_barrier(jnp.mean(values * values, -1)) + EPSILON)

def layer(params, latent_in, skip_in, text_emb, time_emb, cosines, sine_table, key_bias):
    skip_gain, skip_beta, skip_weight, skip_bias, ada_weight, ada_bias, query_key_value_weight, qk_gain, attention_output_weight, out_bias, norm2_gain, norm2_beta, crossed_query_weight, cross_kv_weight, cross_qk_gain, crossed_output_weight, cross_out_bias, norm3_gain, norm3_beta, up_projection_weight, up_bias, down_projection_weight, down_bias = params
    groups = latent_in.shape[0]

    def split_heads(values):
        return values.reshape(groups, values.shape[1], H, HD)
    joined = jnp.concatenate([latent_in, skip_in], -1)
    skip_normed = low(layer_norm(joined) * skip_gain + skip_beta)
    stream = low_back(matmul(skip_normed, skip_weight)) + skip_bias
    shift_vec = matmul(jax.nn.silu(time_emb), ada_weight) + ada_bias
    attn_in = low(layer_norm(stream) + shift_vec[:, None, :])
    q_raw = split_heads(low_back(matmul(attn_in, query_key_value_weight[0])))
    k_raw = split_heads(low_back(matmul(attn_in, query_key_value_weight[1])))
    v_raw = split_heads(low_back(matmul(attn_in, query_key_value_weight[2])))
    query_self = low(rotate(layer_norm(q_raw) * qk_gain[0], cosines, sine_table))
    keys_self = low(rotate(layer_norm(k_raw) * qk_gain[1], cosines, sine_table))
    values_self = low(v_raw)
    self_bias = jnp.zeros((groups, latent_in.shape[1]), jnp.float32)
    attention_combined = low(low_back(attend(query_self, keys_self, values_self, self_bias)))
    branch_one = low_back(matmul(attention_combined, attention_output_weight)) + out_bias
    stream_two = stream + branch_one
    cross_in = low(layer_norm(stream_two) * norm2_gain + norm2_beta)
    qc_raw = split_heads(low_back(matmul(cross_in, crossed_query_weight)))
    kc_raw = split_heads(low_back(matmul(text_emb, cross_kv_weight[0])))
    vc_raw = split_heads(low_back(matmul(text_emb, cross_kv_weight[1])))
    cross_query = low(layer_norm(qc_raw) * cross_qk_gain[0])
    cross_keys = low(layer_norm(kc_raw) * cross_qk_gain[1])
    cross_values = low(vc_raw)
    crossed_combined = low(low_back(attend(cross_query, cross_keys, cross_values, key_bias)))
    branch_two = low_back(matmul(crossed_combined, crossed_output_weight)) + cross_out_bias
    stream_three = stream_two + branch_two
    mlp_in = low(layer_norm(stream_three) * norm3_gain + norm3_beta)
    up_value = low_back(matmul(mlp_in, up_projection_weight)) + up_bias
    hidden_state = low(jax.nn.gelu(up_value, approximate=True))
    branch_three = low_back(matmul(hidden_state, down_projection_weight)) + down_bias
    result = stream_three + branch_three
    stats = jnp.stack([root_mean(stream), root_mean(branch_one), root_mean(branch_two), root_mean(branch_three), root_mean(result)], 1)
    return (result, stats)

def reference(latent_in, skip_in, text_emb, text_length, time_emb, grid_pos, skip_gain, skip_beta, skip_weight, skip_bias, ada_weight, ada_bias, query_key_value_weight, qk_gain, attention_output_weight, out_bias, norm2_gain, norm2_beta, crossed_query_weight, cross_kv_weight, cross_qk_gain, crossed_output_weight, cross_out_bias, norm3_gain, norm3_beta, up_projection_weight, up_bias, down_projection_weight, down_bias, out_grad):
    params = tuple((param.astype(jnp.float32) for param in (skip_gain, skip_beta, skip_weight, skip_bias, ada_weight, ada_bias, query_key_value_weight, qk_gain, attention_output_weight, out_bias, norm2_gain, norm2_beta, crossed_query_weight, cross_kv_weight, cross_qk_gain, crossed_output_weight, cross_out_bias, norm3_gain, norm3_beta, up_projection_weight, up_bias, down_projection_weight, down_bias)))
    group_size = SEQ_DEV
    group_count = latent_in.shape[0] // group_size

    def split_groups(array):
        return array.reshape((group_count, group_size) + array.shape[1:])
    inputs = tuple((split_groups(array) for array in (latent_in, skip_in, text_emb, text_length, time_emb, grid_pos, out_grad)))
    zero_grads = tuple((jnp.zeros_like(param) for param in params))

    def step(running, item):
        latent_part, skip_part, text_part, length_part, time_part, grid_part, grad_part = item
        cosines, sine_table = rope_tables(grid_part)
        key_bias = jnp.where(jnp.arange(TXT)[None, :] < length_part[:, None], 0.0, -1e+30).astype(jnp.float32)

        def run(param_set, latent_val, skip_val, text_val, time_val):
            return layer(param_set, latent_val, skip_val, text_val, time_val, cosines, sine_table, key_bias)
        result, back_fn, stats = jax.vjp(run, params, latent_part.astype(jnp.float32), skip_part.astype(jnp.float32), text_part.astype(jnp.float32), time_part.astype(jnp.float32), has_aux=True)
        grads = back_fn(grad_part.astype(jnp.float32))
        running = tuple((total + grad for total, grad in zip(running, grads[0])))
        return (running, (result.astype(jnp.bfloat16), stats, grads[1], grads[2], grads[3], grads[4]))
    totals, outs = lax.scan(step, zero_grads, inputs)
    merged = tuple((array.reshape((-1,) + array.shape[2:]) for array in outs))
    return (merged[0], merged[1], merged[2], merged[3], merged[4], merged[5]) + totals
```

```python
from functools import partial

import jax
import jax.numpy as jnp
from jax import lax
from jax.sharding import Mesh
from jax.sharding import PartitionSpec as P

HD = 88


EPSILON = 1e-06
ROPE_BASE = 10000.0
PRECISE = lax.Precision.HIGHEST


def layer_norm(values):
    center = values - jnp.mean(values, -1, keepdims=True)
    return center * lax.rsqrt(jnp.mean(center * center, -1, keepdims=True) + EPSILON)


def rope_tables(grid_pos):
    quarter = HD // 4
    frequency = ROPE_BASE ** (-jnp.arange(quarter, dtype=jnp.float32) / quarter)
    row_angle = grid_pos[..., 0:1].astype(jnp.float32) * frequency
    col_angle = grid_pos[..., 1:2].astype(jnp.float32) * frequency
    angles = jnp.concatenate([row_angle, row_angle, col_angle, col_angle], -1)
    return (jnp.cos(angles)[..., None, :], jnp.sin(angles)[..., None, :])


def rotate(values, cosines, sine_table):
    quarter = HD // 4
    first = values[..., :quarter]
    second = values[..., quarter : 2 * quarter]
    third = values[..., 2 * quarter : 3 * quarter]
    fourth = values[..., 3 * quarter :]
    turned = jnp.concatenate([-second, first, -fourth, third], -1)
    return values * cosines + turned * sine_table


def gather_tokens(values):
    return lax.all_gather(values, "tensor", axis=1, tiled=True)


def reduce_tokens(values):
    return lax.psum_scatter(
        values.astype(jnp.bfloat16), "tensor", scatter_dimension=1, tiled=True
    ).astype(jnp.float32)


def attend_forward(query_in, keys_in, values_in, key_bias):
    sequences, length, head_count, head_size = query_in.shape
    block_rows = min(512, length)
    query_blocks = jnp.moveaxis(
        query_in.reshape(sequences, length // block_rows, block_rows, head_count, head_size), 1, 0
    )

    def one_block(portion):
        scores = jnp.einsum(
            "sqhd,skhd->shqk", portion, keys_in, preferred_element_type=jnp.float32
        ) * HD ** (-0.5)
        scores = scores + key_bias[:, None, None, :]
        highest = jnp.max(scores, -1, keepdims=True)
        powers = jnp.exp(scores - highest)
        totals = jnp.sum(powers, -1, keepdims=True)
        weights = (powers / totals).astype(jnp.bfloat16)
        result = jnp.einsum(
            "shqk,skhd->sqhd", weights, values_in, preferred_element_type=jnp.float32
        )
        return (result, (highest + jnp.log(totals))[..., 0])

    results, logsum = lax.map(one_block, query_blocks)
    return (jnp.moveaxis(results, 0, 1).reshape(sequences, length, head_count * head_size), logsum)


def attend_backward(query_in, keys_in, values_in, key_bias, logsum, grad_mixed, result):
    sequences, length, head_count, head_size = query_in.shape
    block_rows = min(512, length)
    grad_heads = grad_mixed.reshape(sequences, length, head_count, head_size)
    delta = jnp.sum(
        grad_heads.astype(jnp.float32) * result.reshape(sequences, length, head_count, head_size),
        -1,
    )

    def cut_rows(array):
        return jnp.moveaxis(
            array.reshape((sequences, length // block_rows, block_rows) + array.shape[2:]), 1, 0
        )

    def one_block(running, item):
        keys_grad, values_grad = running
        portion, lse_part, grad_part, delta_part = item
        scores = jnp.einsum(
            "sqhd,skhd->shqk", portion, keys_in, preferred_element_type=jnp.float32
        ) * HD ** (-0.5)
        scores = scores + key_bias[:, None, None, :]
        weights = jnp.exp(scores - lse_part[..., None])
        values_grad = values_grad + jnp.einsum(
            "shqk,sqhd->skhd",
            weights.astype(jnp.bfloat16),
            grad_part,
            preferred_element_type=jnp.float32,
        )
        weight_grad = jnp.einsum(
            "sqhd,skhd->shqk", grad_part, values_in, preferred_element_type=jnp.float32
        )
        score_grad = (weights * (weight_grad - jnp.swapaxes(delta_part, 1, 2)[..., None])).astype(
            jnp.bfloat16
        )
        query_grad = jnp.einsum(
            "shqk,skhd->sqhd", score_grad, keys_in, preferred_element_type=jnp.float32
        ) * HD ** (-0.5)
        keys_grad = keys_grad + jnp.einsum(
            "shqk,sqhd->skhd", score_grad, portion, preferred_element_type=jnp.float32
        ) * HD ** (-0.5)
        return ((keys_grad, values_grad), query_grad)

    zero_keys = jnp.zeros(keys_in.shape, jnp.float32)
    (keys_grad, values_grad), query_grad = lax.scan(
        one_block,
        (zero_keys, zero_keys),
        (cut_rows(query_in), logsum, cut_rows(grad_heads), cut_rows(delta)),
    )
    query_grad = jnp.moveaxis(query_grad, 0, 1).reshape(query_in.shape)
    return (query_grad, keys_grad, values_grad)


def affine_norm(values, gain, beta):
    return layer_norm(values) * gain + beta


def tensor_local(
    latent_in,
    skip_in,
    text_emb,
    text_length,
    time_emb,
    grid_pos,
    skip_gain,
    skip_beta,
    skip_weight,
    skip_bias,
    ada_weight,
    ada_bias,
    query_key_value_weight,
    qk_gain,
    attention_output_weight,
    out_bias,
    norm2_gain,
    norm2_beta,
    crossed_query_weight,
    cross_kv_weight,
    cross_qk_gain,
    crossed_output_weight,
    cross_out_bias,
    norm3_gain,
    norm3_beta,
    up_projection_weight,
    up_bias,
    down_projection_weight,
    down_bias,
    out_grad,
):
    tensor_count = lax.axis_size("tensor")
    tensor_rank = lax.axis_index("tensor")
    sequences, local_len, model_width = latent_in.shape
    full_len = local_len * tensor_count
    col_width = ada_weight.shape[1]
    head_cols = query_key_value_weight.shape[2]
    local_heads = head_cols // HD
    cosines, sine_table = rope_tables(grid_pos)
    key_bias = jnp.where(
        jnp.arange(text_emb.shape[1])[None, :] < text_length[:, None], 0.0, -1e30
    ).astype(jnp.float32)
    self_bias = jnp.zeros((sequences, full_len), jnp.float32)
    skip_gain_f = skip_gain.astype(jnp.float32)
    skip_beta_f = skip_beta.astype(jnp.float32)
    norm2_gain_f = norm2_gain.astype(jnp.float32)
    norm2_beta_f = norm2_beta.astype(jnp.float32)
    norm3_gain_f = norm3_gain.astype(jnp.float32)
    norm3_beta_f = norm3_beta.astype(jnp.float32)
    qk_gain_f = qk_gain.astype(jnp.float32)
    cross_gain_f = cross_qk_gain.astype(jnp.float32)

    def first_norm(stream_in, shift_in):
        return layer_norm(stream_in) + shift_in[:, None, :]

    def qk_prep(raw, gain):
        return rotate(
            layer_norm(raw.reshape(sequences, full_len, local_heads, HD)) * gain,
            cosines,
            sine_table,
        )

    def head_norm(raw, gain):
        return layer_norm(raw.reshape(raw.shape[0], raw.shape[1], local_heads, HD)) * gain

    joined = jnp.concatenate([latent_in.astype(jnp.float32), skip_in.astype(jnp.float32)], -1)
    skip_normed = affine_norm(joined, skip_gain_f, skip_beta_f).astype(jnp.bfloat16)
    skip_all = gather_tokens(skip_normed)
    skip_cols = jnp.einsum(
        "slc,ce->sle", skip_all, skip_weight, preferred_element_type=jnp.float32
    ) + skip_bias.astype(jnp.float32)
    stream = lax.all_to_all(
        skip_cols.astype(jnp.bfloat16), "tensor", split_axis=1, concat_axis=2, tiled=True
    ).astype(skip_cols.dtype)
    condition = jax.nn.silu(time_emb.astype(jnp.float32))
    ada_weight_f = ada_weight.astype(jnp.float32)
    shift_part = jnp.dot(condition, ada_weight_f, precision=PRECISE) + ada_bias.astype(jnp.float32)
    shift_vec = lax.all_gather(shift_part, "tensor", axis=1, tiled=True)
    attn_in = first_norm(stream, shift_vec).astype(jnp.bfloat16)
    attention_gathered = gather_tokens(attn_in)
    projected = jnp.einsum(
        "mxp,jpc->jmxc",
        attention_gathered,
        query_key_value_weight,
        preferred_element_type=jnp.float32,
    )
    query_self = qk_prep(projected[0], qk_gain_f[0]).astype(jnp.bfloat16)
    keys_self = qk_prep(projected[1], qk_gain_f[1]).astype(jnp.bfloat16)
    values_self = projected[2].reshape(sequences, full_len, local_heads, HD).astype(jnp.bfloat16)
    attn_result, attn_logsum = attend_forward(query_self, keys_self, values_self, self_bias)
    attention_combined = attn_result.astype(jnp.bfloat16)
    branch_one = reduce_tokens(
        jnp.einsum(
            "jpe,ec->jpc",
            attention_combined,
            attention_output_weight,
            preferred_element_type=jnp.float32,
        )
    ) + out_bias.astype(jnp.float32)
    stream_two = stream + branch_one
    cross_in = affine_norm(stream_two, norm2_gain_f, norm2_beta_f).astype(jnp.bfloat16)
    crossed_gathered = gather_tokens(cross_in)
    query_raw = jnp.einsum(
        "pik,kx->pix", crossed_gathered, crossed_query_weight, preferred_element_type=jnp.float32
    )
    text_proj = jnp.einsum(
        "std,kdh->ksth", text_emb, cross_kv_weight, preferred_element_type=jnp.float32
    )
    cross_query = head_norm(query_raw, cross_gain_f[0]).astype(jnp.bfloat16)
    cross_keys = head_norm(text_proj[0], cross_gain_f[1]).astype(jnp.bfloat16)
    cross_values = (
        text_proj[1].reshape(sequences, text_proj.shape[2], local_heads, HD).astype(jnp.bfloat16)
    )
    cross_result, cross_logsum = attend_forward(cross_query, cross_keys, cross_values, key_bias)
    crossed_combined = cross_result.astype(jnp.bfloat16)
    branch_two = reduce_tokens(
        jnp.einsum(
            "jpe,ec->jpc",
            crossed_combined,
            crossed_output_weight,
            preferred_element_type=jnp.float32,
        )
    ) + cross_out_bias.astype(jnp.float32)
    stream_three = stream_two + branch_two
    mlp_in = affine_norm(stream_three, norm3_gain_f, norm3_beta_f).astype(jnp.bfloat16)
    gelu_fn = partial(jax.nn.gelu, approximate=True)
    perceptron_gathered = gather_tokens(mlp_in)
    hidden_pre = jnp.einsum(
        "ctk,kr->ctr", perceptron_gathered, up_projection_weight, preferred_element_type=jnp.float32
    ) + up_bias.astype(jnp.float32)
    hidden_state = gelu_fn(hidden_pre).astype(jnp.bfloat16)
    branch_three = reduce_tokens(
        jnp.einsum(
            "jgy,yv->jgv", hidden_state, down_projection_weight, preferred_element_type=jnp.float32
        )
    ) + down_bias.astype(jnp.float32)
    output = stream_three + branch_three
    stats = jnp.stack(
        [
            jnp.sqrt(jnp.mean(stream_term * stream_term, -1) + EPSILON)
            for stream_term in (stream, branch_one, branch_two, branch_three, output)
        ],
        1,
    )
    grad_out = out_grad.astype(jnp.float32)
    down_bias_part = jnp.sum(grad_out, axis=(0, 1))
    _, gelu_back = jax.vjp(gelu_fn, hidden_pre)
    gradient_gathered = gather_tokens(out_grad)
    hidden_grad = jnp.einsum(
        "bcq,eq->bce", gradient_gathered, down_projection_weight, preferred_element_type=jnp.float32
    )
    down_weight_grad = jnp.einsum(
        "mho,mhj->oj", hidden_state, gradient_gathered, preferred_element_type=jnp.float32
    )
    pre_grad = gelu_back(hidden_grad)[0]
    up_bias_grad = jnp.sum(pre_grad, axis=(0, 1))
    prenorm_reduced = pre_grad.astype(jnp.bfloat16)
    up_projection_gradient = jnp.einsum(
        "boy,bot->yt", perceptron_gathered, prenorm_reduced, preferred_element_type=jnp.float32
    )
    norm3_grad_in = reduce_tokens(
        jnp.einsum(
            "tke,ve->tkv", prenorm_reduced, up_projection_weight, preferred_element_type=jnp.float32
        )
    )
    _, norm3_back = jax.vjp(affine_norm, stream_three, norm3_gain_f, norm3_beta_f)
    from_three, gain3_part, beta3_part = norm3_back(norm3_grad_in)
    grad_three = grad_out + from_three
    cross_bias_part = jnp.sum(grad_three, axis=(0, 1))
    gradient_third_gathered = gather_tokens(grad_three.astype(jnp.bfloat16))
    cross_out_weight_grad = jnp.einsum(
        "kwy,kwn->yn", crossed_combined, gradient_third_gathered, preferred_element_type=jnp.float32
    )
    cross_mixed_grad = jnp.einsum(
        "ofz,iz->ofi",
        gradient_third_gathered,
        crossed_output_weight,
        preferred_element_type=jnp.float32,
    ).astype(jnp.bfloat16)
    cq_grad, ck_grad, cv_grad = attend_backward(
        cross_query,
        cross_keys,
        cross_values,
        key_bias,
        cross_logsum,
        cross_mixed_grad,
        cross_result,
    )
    _, cq_back = jax.vjp(head_norm, query_raw, cross_gain_f[0])
    query_raw_grad, cq_gain_part = cq_back(cq_grad)
    _, ck_back = jax.vjp(head_norm, text_proj[0], cross_gain_f[1])
    keys_raw_grad, ck_gain_part = ck_back(ck_grad)
    cross_gain_part = jnp.stack([cq_gain_part, ck_gain_part])
    query_reduced = query_raw_grad.astype(jnp.bfloat16)
    cross_query_weight_grad = jnp.einsum(
        "yfw,yfb->wb", crossed_gathered, query_reduced, preferred_element_type=jnp.float32
    )
    text_grads = jnp.stack(
        [keys_raw_grad, cv_grad.reshape(sequences, cv_grad.shape[1], head_cols)]
    ).astype(jnp.bfloat16)
    cross_kv_weight_grad = jnp.einsum(
        "std,ksth->kdh", text_emb, text_grads, preferred_element_type=jnp.float32
    )
    text_part = jnp.einsum(
        "ksth,kdh->std", text_grads, cross_kv_weight, preferred_element_type=jnp.float32
    )
    norm2_grad_in = reduce_tokens(
        jnp.einsum(
            "rjc,vc->rjv", query_reduced, crossed_query_weight, preferred_element_type=jnp.float32
        )
    )
    _, norm2_back = jax.vjp(affine_norm, stream_two, norm2_gain_f, norm2_beta_f)
    from_two, gain2_part, beta2_part = norm2_back(norm2_grad_in)
    grad_two = grad_three + from_two
    out_bias_part = jnp.sum(grad_two, axis=(0, 1))
    gradient_second_gathered = gather_tokens(grad_two.astype(jnp.bfloat16))
    out_weight_grad = jnp.einsum(
        "kwy,kwn->yn",
        attention_combined,
        gradient_second_gathered,
        preferred_element_type=jnp.float32,
    )
    attn_mixed_grad = jnp.einsum(
        "ofz,iz->ofi",
        gradient_second_gathered,
        attention_output_weight,
        preferred_element_type=jnp.float32,
    ).astype(jnp.bfloat16)
    sq_grad, sk_grad, sv_grad = attend_backward(
        query_self, keys_self, values_self, self_bias, attn_logsum, attn_mixed_grad, attn_result
    )
    _, sq_back = jax.vjp(qk_prep, projected[0], qk_gain_f[0])
    q_raw_grad, sq_gain_part = sq_back(sq_grad)
    _, sk_back = jax.vjp(qk_prep, projected[1], qk_gain_f[1])
    k_raw_grad, sk_gain_part = sk_back(sk_grad)
    self_gain_part = jnp.stack([sq_gain_part, sk_gain_part])
    projection_gradient = jnp.stack(
        [q_raw_grad, k_raw_grad, sv_grad.reshape(sequences, full_len, head_cols)]
    ).astype(jnp.bfloat16)
    qkv_weight_grad = jnp.einsum(
        "yze,myzi->mei", attention_gathered, projection_gradient, preferred_element_type=jnp.float32
    )
    first_grad_in = reduce_tokens(
        jnp.einsum(
            "apwf,acf->pwc",
            projection_gradient,
            query_key_value_weight,
            preferred_element_type=jnp.float32,
        )
    )
    _, first_back = jax.vjp(first_norm, stream, shift_vec)
    from_one, shift_part_grad = first_back(first_grad_in)
    grad_one = grad_two + from_one
    (
        shift_grad,
        down_bias_sum,
        gain3_sum,
        beta3_sum,
        cross_bias_sum,
        gain2_sum,
        beta2_sum,
        cross_gain_sum,
        out_bias_sum,
        self_gain_sum,
    ) = (
        lax.psum(shift_part_grad.astype(jnp.bfloat16), "tensor").astype(jnp.float32),
        lax.psum(down_bias_part.astype(jnp.bfloat16), "tensor").astype(jnp.float32),
        lax.psum(gain3_part.astype(jnp.bfloat16), "tensor").astype(jnp.float32),
        lax.psum(beta3_part.astype(jnp.bfloat16), "tensor").astype(jnp.float32),
        lax.psum(cross_bias_part.astype(jnp.bfloat16), "tensor").astype(jnp.float32),
        lax.psum(gain2_part.astype(jnp.bfloat16), "tensor").astype(jnp.float32),
        lax.psum(beta2_part.astype(jnp.bfloat16), "tensor").astype(jnp.float32),
        lax.psum(cross_gain_part.astype(jnp.bfloat16), "tensor").astype(jnp.float32),
        lax.psum(out_bias_part.astype(jnp.bfloat16), "tensor").astype(jnp.float32),
        lax.psum(self_gain_part.astype(jnp.bfloat16), "tensor").astype(jnp.float32),
    )
    shift_cols = lax.dynamic_slice_in_dim(shift_grad, tensor_rank * col_width, col_width, 1)
    ada_bias_grad = jnp.sum(shift_cols, axis=0)
    ada_weight_grad = jnp.dot(condition.T, shift_cols, precision=PRECISE)
    condition_grad = jnp.dot(shift_cols, ada_weight_f.T, precision=PRECISE)
    _, silu_back = jax.vjp(jax.nn.silu, time_emb.astype(jnp.float32))
    time_part = silu_back(condition_grad)[0]
    skip_grad_cols = lax.all_to_all(
        grad_one.astype(jnp.bfloat16), "tensor", split_axis=2, concat_axis=1, tiled=True
    ).astype(grad_one.dtype)
    skip_bias_grad = jnp.sum(skip_grad_cols, axis=(0, 1))
    skip_low = skip_grad_cols.astype(jnp.bfloat16)
    skip_weight_grad = jnp.einsum(
        "slc,sle->ce", skip_all, skip_low, preferred_element_type=jnp.float32
    )
    joined_grad_in = reduce_tokens(
        jnp.einsum("sle,ce->slc", skip_low, skip_weight, preferred_element_type=jnp.float32)
    )
    _, skip_norm_back = jax.vjp(affine_norm, joined, skip_gain_f, skip_beta_f)
    joined_grad, skip_gain_part, skip_beta_part = skip_norm_back(joined_grad_in)
    latent_grad = joined_grad[..., :model_width]
    skip_grad = joined_grad[..., model_width:]
    text_grad, time_grad, skip_gain_sum, skip_beta_sum = (
        lax.psum(text_part.astype(jnp.bfloat16), "tensor").astype(jnp.float32),
        lax.psum(time_part.astype(jnp.bfloat16), "tensor").astype(jnp.float32),
        lax.psum(skip_gain_part.astype(jnp.bfloat16), "tensor").astype(jnp.float32),
        lax.psum(skip_beta_part.astype(jnp.bfloat16), "tensor").astype(jnp.float32),
    )
    weight_sums = (
        lax.psum(skip_gain_sum.astype(jnp.bfloat16), "dp").astype(jnp.float32),
        lax.psum(skip_beta_sum.astype(jnp.bfloat16), "dp").astype(jnp.float32),
        lax.psum(skip_weight_grad.astype(jnp.bfloat16), "dp").astype(jnp.float32),
        lax.psum(skip_bias_grad.astype(jnp.bfloat16), "dp").astype(jnp.float32),
        lax.psum(ada_weight_grad.astype(jnp.bfloat16), "dp").astype(jnp.float32),
        lax.psum(ada_bias_grad.astype(jnp.bfloat16), "dp").astype(jnp.float32),
        lax.psum(qkv_weight_grad.astype(jnp.bfloat16), "dp").astype(jnp.float32),
        lax.psum(self_gain_sum.astype(jnp.bfloat16), "dp").astype(jnp.float32),
        lax.psum(out_weight_grad.astype(jnp.bfloat16), "dp").astype(jnp.float32),
        lax.psum(out_bias_sum.astype(jnp.bfloat16), "dp").astype(jnp.float32),
        lax.psum(gain2_sum.astype(jnp.bfloat16), "dp").astype(jnp.float32),
        lax.psum(beta2_sum.astype(jnp.bfloat16), "dp").astype(jnp.float32),
        lax.psum(cross_query_weight_grad.astype(jnp.bfloat16), "dp").astype(jnp.float32),
        lax.psum(cross_kv_weight_grad.astype(jnp.bfloat16), "dp").astype(jnp.float32),
        lax.psum(cross_gain_sum.astype(jnp.bfloat16), "dp").astype(jnp.float32),
        lax.psum(cross_out_weight_grad.astype(jnp.bfloat16), "dp").astype(jnp.float32),
        lax.psum(cross_bias_sum.astype(jnp.bfloat16), "dp").astype(jnp.float32),
        lax.psum(gain3_sum.astype(jnp.bfloat16), "dp").astype(jnp.float32),
        lax.psum(beta3_sum.astype(jnp.bfloat16), "dp").astype(jnp.float32),
        lax.psum(up_projection_gradient.astype(jnp.bfloat16), "dp").astype(jnp.float32),
        lax.psum(up_bias_grad.astype(jnp.bfloat16), "dp").astype(jnp.float32),
        lax.psum(down_weight_grad.astype(jnp.bfloat16), "dp").astype(jnp.float32),
        lax.psum(down_bias_sum.astype(jnp.bfloat16), "dp").astype(jnp.float32),
    )
    return (
        output.astype(jnp.bfloat16),
        stats,
        latent_grad,
        skip_grad,
        text_grad,
        time_grad,
    ) + tuple(weight_sums)


def ring_pairs(size, step):
    return [(rank, (rank + step) % size) for rank in range(size)]


def swap_cores(values):
    return lax.ppermute(values, "core", [(0, 1), (1, 0)])


def from_later(values, step, size):
    return lax.ppermute(values, "tensor", ring_pairs(size, -step))


def from_earlier(values, step, size):
    return lax.ppermute(values, "tensor", ring_pairs(size, step))


def spread_pairs(size, turn):
    pairs = []
    for core in range(2):
        for rank in range(size):
            piece = (rank + turn) % size
            pairs.append((core * size + rank, (piece % 2) * size + 2 * core + piece // 2))
    return pairs


def pick(array, index):
    return lax.dynamic_index_in_dim(array, index, 0, keepdims=False)


def rolled(array, start):
    return lax.dynamic_slice_in_dim(jnp.concatenate([array, array], 0), start, array.shape[0], 0)


def dot_tt(left, right):
    return lax.dot_general(left, right, (((1,), (1,)), ((), ())), preferred_element_type=jnp.float32)


def dot_nn(left, right):
    return lax.dot_general(left, right, (((1,), (0,)), ((), ())), preferred_element_type=jnp.float32)


def dot_tn(left, right):
    return lax.dot_general(left, right, (((0,), (0,)), ((), ())), preferred_element_type=jnp.float32)


def chip_local(
    latent_in,
    skip_in,
    text_emb,
    text_length,
    time_emb,
    grid_pos,
    skip_gain,
    skip_beta,
    skip_weight,
    skip_bias,
    ada_weight,
    ada_bias,
    query_key_value_weight,
    qk_gain,
    attention_output_weight,
    out_bias,
    norm2_gain,
    norm2_beta,
    crossed_query_weight,
    cross_kv_weight,
    cross_qk_gain,
    crossed_output_weight,
    cross_out_bias,
    norm3_gain,
    norm3_beta,
    up_projection_weight,
    up_bias,
    down_projection_weight,
    down_bias,
    out_grad,
):
    f32 = jnp.float32
    low = jnp.bfloat16
    size = lax.axis_size("tensor")
    chips = lax.axis_size("chip")
    rank = lax.axis_index("tensor")
    core = lax.axis_index("core")
    chip = lax.axis_index("chip")
    sequences, local_len, width = latent_in.shape
    piece_len = local_len // 2
    own_len = size * piece_len
    shard = ada_weight.shape[1]
    half = shard // 2
    heads = size * half // HD
    ff_half = up_bias.shape[0] // 2
    ff_part = ff_half // chips
    at_home = core == rank // sequences

    def spread(values):
        return jnp.stack(
            [
                lax.ppermute(
                    pick(values, (rank + turn) % size), ("core", "tensor"), spread_pairs(size, turn)
                )
                for turn in range(size)
            ]
        )

    def collect(values):
        parts = [
            lax.ppermute(
                values[turn],
                ("core", "tensor"),
                [(target, source) for source, target in spread_pairs(size, turn)],
            )
            for turn in range(size)
        ]
        return rolled(jnp.stack(parts), (size - rank) % size)

    def of_sequence(values):
        mine = pick(values, rank % sequences)
        return jnp.where(at_home, mine, swap_cores(mine))

    def both(values):
        return jnp.concatenate([values, swap_cores(values)], 0)

    def halve(values):
        return values[:own_len] + swap_cores(values[own_len:].astype(low)).astype(f32)

    def gather_rows(own):
        mine = pick(own, chip)
        later = jnp.stack([from_later(mine, step, size) for step in range(1, size)])
        rest = lax.all_gather(later, "chip", axis=0, tiled=False)
        return jnp.concatenate([own[:, None], rest], 1)

    def reduce_rows(partial_sums):
        rows = partial_sums.shape[2]
        parts = lax.psum_scatter(
            partial_sums.reshape(chips * size * rows, width), "chip", scatter_dimension=0, tiled=True
        ).reshape(size, rows, width)
        total = parts[0].astype(f32)
        for step in range(1, size):
            total = total + from_earlier(parts[step], step, size).astype(f32)
        own = lax.all_gather(total.astype(low), "chip", axis=0, tiled=True)
        own = own.reshape(chips, rows, width)
        other = swap_cores(own)
        return jnp.where(core == 0, own, other), jnp.where(core == 0, other, own)

    def half_cols(weight):
        return lax.dynamic_slice_in_dim(weight, core * half, half, 1).T

    def half_rows(weight):
        return lax.dynamic_slice_in_dim(weight, core * half, half, 0)

    skip_half = lax.dynamic_slice_in_dim(skip_weight, core * width, width, 0).T
    skip_part = shard // chips
    skip_mine = pick(skip_half.reshape(chips, skip_part, width), chip)
    skip_rel = jnp.stack([skip_mine] + [from_later(skip_mine, step, size) for step in range(1, size)])
    skip_abs = rolled(skip_rel, (size - rank) % size)
    skip_own_w = (
        lax.all_gather(skip_abs, "chip", axis=0, tiled=False)
        .transpose(1, 0, 2, 3)
        .reshape(width, width)
    )
    skip_other_w = swap_cores(skip_own_w)

    self_own = jnp.stack(
        [half_cols(query_key_value_weight[i]) for i in range(3)]
        + [half_rows(attention_output_weight)]
    )
    self_full = gather_rows(self_own).reshape(4, size * half, width)
    cross_own = jnp.stack(
        [half_cols(crossed_query_weight), half_cols(cross_kv_weight[0]), half_cols(cross_kv_weight[1])]
        + [half_rows(crossed_output_weight)]
    )
    cross_full = gather_rows(cross_own).reshape(4, size * half, width)
    up_own = lax.dynamic_slice_in_dim(up_projection_weight, core * ff_half, ff_half, 1).T
    up_full = gather_rows(up_own.reshape(chips, ff_part, width)).reshape(size * ff_half, width)
    down_own = lax.dynamic_slice_in_dim(down_projection_weight, core * ff_half, ff_half, 0)
    down_full = gather_rows(down_own.reshape(chips, ff_part, width)).reshape(size * ff_half, width)

    condition = jax.nn.silu(time_emb.astype(f32))
    ada_weight_f = ada_weight.astype(f32)
    shift_part = jnp.dot(condition, ada_weight_f, precision=PRECISE) + ada_bias.astype(f32)
    small = jnp.concatenate([shift_part, skip_bias.astype(f32)[None]], 0)
    small_all = rolled(
        jnp.stack([small] + [from_later(small, step, size) for step in range(1, size)]),
        (size - rank) % size,
    )
    small_all = small_all.transpose(1, 0, 2).reshape(sequences + 1, width)
    skip_bias_f = small_all[sequences]
    shift_length = of_sequence(
        jnp.concatenate([small_all[:sequences], text_length.astype(f32)[:, None]], 1)
    )
    shift_vec = shift_length[:width]
    own_length = shift_length[width]
    up_bias_own = lax.dynamic_slice_in_dim(up_bias, core * ff_half, ff_half, 0)
    up_bias_f = (
        jnp.stack([up_bias_own] + [from_later(up_bias_own, step, size) for step in range(1, size)])
        .reshape(size, chips, ff_part)
        .transpose(1, 0, 2)
        .reshape(size * ff_half)
        .astype(f32)
    )
    text_own = of_sequence(text_emb)
    positions = of_sequence(grid_pos)
    text_size = text_own.shape[0]
    key_bias = jnp.where(jnp.arange(text_size)[None, :] < own_length, 0.0, -1e30).astype(f32)

    by_piece = positions.reshape(2 * size, piece_len, 2)

    def piece_index(of_core, turn):
        source = (2 * (rank % 2) + of_core - turn) % size
        return source * 2 + of_core

    ordered = jnp.concatenate(
        [pick(by_piece, piece_index(of_core, turn)) for of_core in (core, 1 - core) for turn in range(size)],
        0,
    )
    cosines, sine_table = rope_tables(ordered)

    skip_gain_f = skip_gain.astype(f32)
    skip_beta_f = skip_beta.astype(f32)
    norm2_gain_f = norm2_gain.astype(f32)
    norm2_beta_f = norm2_beta.astype(f32)
    norm3_gain_f = norm3_gain.astype(f32)
    norm3_beta_f = norm3_beta.astype(f32)
    qk_gain_f = qk_gain.astype(f32)
    cross_gain_f = cross_qk_gain.astype(f32)

    def first_norm(stream_in, shift_in):
        return layer_norm(stream_in) + shift_in[None, :]

    def qk_prep(raw, gain):
        return rotate(layer_norm(raw.reshape(raw.shape[0], heads, HD)) * gain, cosines, sine_table)

    def head_norm(raw, gain):
        return layer_norm(raw.reshape(raw.shape[0], heads, HD)) * gain

    latent_f = latent_in.reshape(own_len, width).astype(f32)
    skip_f = skip_in.reshape(own_len, width).astype(f32)
    joined_size = 2 * width
    center = (jnp.sum(latent_f, -1, keepdims=True) + jnp.sum(skip_f, -1, keepdims=True)) / joined_size
    latent_c = latent_f - center
    skip_c = skip_f - center
    spread_sq = jnp.sum(latent_c * latent_c, -1, keepdims=True) + jnp.sum(
        skip_c * skip_c, -1, keepdims=True
    )
    inverse = lax.rsqrt(spread_sq / joined_size + EPSILON)
    normed = jnp.stack(
        [
            (latent_c * inverse * skip_gain_f[:width] + skip_beta_f[:width]).astype(low),
            (skip_c * inverse * skip_gain_f[width:] + skip_beta_f[width:]).astype(low),
        ]
    )
    normed_own = pick(normed, core)
    normed_other = pick(normed, 1 - core)
    stream_home = (
        dot_tt(normed_own, skip_own_w) + dot_tt(normed_other, skip_other_w) + skip_bias_f
    ).astype(low)
    stream = spread(stream_home.reshape(size, piece_len, width)).reshape(own_len, width).astype(f32)
    grad_low = spread(out_grad.reshape(size, piece_len, width)).reshape(own_len, width)

    attn_in = both(first_norm(stream, shift_vec).astype(low))
    projected = [dot_tt(attn_in, self_full[i]) for i in range(3)]
    query_self = qk_prep(projected[0], qk_gain_f[0]).astype(low)[None]
    keys_self = qk_prep(projected[1], qk_gain_f[1]).astype(low)[None]
    values_self = projected[2].reshape(1, 2 * own_len, heads, HD).astype(low)
    self_bias = jnp.zeros((1, 2 * own_len), f32)
    attn_result, attn_logsum = attend_forward(query_self, keys_self, values_self, self_bias)
    attention_combined = attn_result[0].astype(low)
    branch_one = halve(dot_nn(attention_combined, self_full[3])) + out_bias.astype(f32)
    stream_two = stream + branch_one
    cross_in = both(affine_norm(stream_two, norm2_gain_f, norm2_beta_f).astype(low))
    query_raw = dot_tt(cross_in, cross_full[0])
    keys_raw = dot_tt(text_own, cross_full[1])
    values_raw = dot_tt(text_own, cross_full[2])
    cross_query = head_norm(query_raw, cross_gain_f[0]).astype(low)[None]
    cross_keys = head_norm(keys_raw, cross_gain_f[1]).astype(low)[None]
    cross_values = values_raw.reshape(1, text_size, heads, HD).astype(low)
    cross_result, cross_logsum = attend_forward(cross_query, cross_keys, cross_values, key_bias)
    crossed_combined = cross_result[0].astype(low)
    branch_two = halve(dot_nn(crossed_combined, cross_full[3])) + cross_out_bias.astype(f32)
    stream_three = stream_two + branch_two
    mlp_in = both(affine_norm(stream_three, norm3_gain_f, norm3_beta_f).astype(low))
    gelu_fn = partial(jax.nn.gelu, approximate=True)
    hidden_pre = dot_tt(mlp_in, up_full) + up_bias_f
    hidden_state, gelu_back = jax.vjp(gelu_fn, hidden_pre)
    hidden_state = hidden_state.astype(low)
    branch_three = halve(dot_nn(hidden_state, down_full)) + down_bias.astype(f32)
    output = stream_three + branch_three
    stats = jnp.stack(
        [
            jnp.sqrt(jnp.mean(term * term, -1) + EPSILON)
            for term in (stream, branch_one, branch_two, branch_three, output)
        ]
    )
    output_home = collect(output.astype(low).reshape(size, piece_len, width)).reshape(latent_in.shape)
    stats_home = (
        collect(stats.reshape(5, size, piece_len).transpose(1, 0, 2))
        .reshape(sequences, 2, 5, piece_len)
        .transpose(0, 2, 1, 3)
        .reshape(sequences, 5, local_len)
    )

    grad_out = grad_low.astype(f32)
    down_bias_part = jnp.sum(grad_out, axis=0)
    grad_all = both(grad_low)
    down_grad = dot_tn(hidden_state, grad_all).astype(low)
    hidden_grad = dot_tt(grad_all, down_full)
    pre_grad = gelu_back(hidden_grad)[0]
    up_bias_part = jnp.sum(pre_grad, axis=0)
    pre_low = pre_grad.astype(low)
    norm3_grad_in = halve(dot_nn(pre_low, up_full))
    up_grad = dot_tn(pre_low, mlp_in).astype(low)
    _, norm3_back = jax.vjp(affine_norm, stream_three, norm3_gain_f, norm3_beta_f)
    from_three, gain3_part, beta3_part = norm3_back(norm3_grad_in)
    grad_three = grad_out + from_three
    cross_bias_part = jnp.sum(grad_three, axis=0)
    three_all = both(grad_three.astype(low))
    cross_out_grad = dot_tn(crossed_combined, three_all).astype(low)
    cross_mixed_grad = dot_tt(three_all, cross_full[3]).astype(low)[None]
    cq_grad, ck_grad, cv_grad = attend_backward(
        cross_query, cross_keys, cross_values, key_bias, cross_logsum, cross_mixed_grad, cross_result
    )
    _, cq_back = jax.vjp(head_norm, query_raw, cross_gain_f[0])
    query_raw_grad, cq_gain_part = cq_back(cq_grad[0])
    _, ck_back = jax.vjp(head_norm, keys_raw, cross_gain_f[1])
    keys_raw_grad, ck_gain_part = ck_back(ck_grad[0])
    cross_gain_part = jnp.concatenate([cq_gain_part, ck_gain_part])
    query_low = query_raw_grad.astype(low)
    keys_low = keys_raw_grad.astype(low)
    values_low = cv_grad.reshape(text_size, size * half).astype(low)
    norm2_grad_in = halve(dot_nn(query_low, cross_full[0]))
    cross_grads = jnp.stack(
        [
            dot_tn(query_low, cross_in).astype(low),
            dot_tn(keys_low, text_own).astype(low),
            dot_tn(values_low, text_own).astype(low),
            cross_out_grad,
        ]
    )
    text_part = dot_nn(keys_low, cross_full[1]) + dot_nn(values_low, cross_full[2])
    _, norm2_back = jax.vjp(affine_norm, stream_two, norm2_gain_f, norm2_beta_f)
    from_two, gain2_part, beta2_part = norm2_back(norm2_grad_in)
    grad_two = grad_three + from_two
    out_bias_part = jnp.sum(grad_two, axis=0)
    two_all = both(grad_two.astype(low))
    out_weight_part = dot_tn(attention_combined, two_all).astype(low)
    attn_mixed_grad = dot_tt(two_all, self_full[3]).astype(low)[None]
    sq_grad, sk_grad, sv_grad = attend_backward(
        query_self, keys_self, values_self, self_bias, attn_logsum, attn_mixed_grad, attn_result
    )
    _, sq_back = jax.vjp(qk_prep, projected[0], qk_gain_f[0])
    q_raw_grad, sq_gain_part = sq_back(sq_grad[0])
    _, sk_back = jax.vjp(qk_prep, projected[1], qk_gain_f[1])
    k_raw_grad, sk_gain_part = sk_back(sk_grad[0])
    self_gain_part = jnp.concatenate([sq_gain_part, sk_gain_part])
    proj_grads = [
        q_raw_grad.astype(low),
        k_raw_grad.astype(low),
        sv_grad.reshape(2 * own_len, size * half).astype(low),
    ]
    first_grad_in = halve(
        dot_nn(proj_grads[0], self_full[0])
        + dot_nn(proj_grads[1], self_full[1])
        + dot_nn(proj_grads[2], self_full[2])
    )
    self_grads = jnp.stack(
        [dot_tn(grad, attn_in).astype(low) for grad in proj_grads] + [out_weight_part]
    )
    _, first_back = jax.vjp(first_norm, stream, shift_vec)
    from_one, shift_own_grad = first_back(first_grad_in)
    grad_one = (grad_two + from_one).astype(low)

    home_grad = collect(grad_one.reshape(size, piece_len, width)).reshape(own_len, width)
    skip_bias_part = jnp.sum(home_grad.astype(f32), axis=0)
    skip_own_grad = dot_tn(home_grad, normed_own)
    skip_other_grad = dot_tn(home_grad, normed_other).astype(low)
    skip_sum = (skip_own_grad + swap_cores(skip_other_grad).astype(f32)).astype(low)
    own_in = dot_nn(home_grad, skip_own_w)
    other_in = dot_nn(home_grad, skip_other_w)
    latent_in_grad = jnp.where(core == 0, own_in, other_in)
    skip_in_grad = jnp.where(core == 0, other_in, own_in)
    latent_ln = latent_c * inverse
    skip_ln = skip_c * inverse
    skip_gain_part = jnp.concatenate(
        [jnp.sum(latent_in_grad * latent_ln, 0), jnp.sum(skip_in_grad * skip_ln, 0)]
    )
    skip_beta_part = jnp.concatenate([jnp.sum(latent_in_grad, 0), jnp.sum(skip_in_grad, 0)])
    latent_h = latent_in_grad * skip_gain_f[:width]
    skip_h = skip_in_grad * skip_gain_f[width:]
    mean_h = (jnp.sum(latent_h, -1, keepdims=True) + jnp.sum(skip_h, -1, keepdims=True)) / joined_size
    mean_hl = (
        jnp.sum(latent_h * latent_ln, -1, keepdims=True)
        + jnp.sum(skip_h * skip_ln, -1, keepdims=True)
    ) / joined_size
    latent_grad = (inverse * (latent_h - mean_h - latent_ln * mean_hl)).reshape(latent_in.shape)
    skip_grad = (inverse * (skip_h - mean_h - skip_ln * mean_hl)).reshape(latent_in.shape)

    shift_own = shift_own_grad + swap_cores(shift_own_grad)
    shift_all = lax.all_gather(shift_own, ("chip", "tensor"), axis=0, tiled=False)
    condition_all = jax.nn.silu(
        lax.all_gather(time_emb, ("chip", "core"), axis=0, tiled=True).astype(f32)
    )
    shift_cols = lax.dynamic_slice_in_dim(shift_all, rank * shard, shard, 1)
    ada_bias_grad = jnp.sum(shift_cols, axis=0)
    ada_weight_grad = jnp.dot(condition_all.T, shift_cols, precision=PRECISE)
    shift_mine = lax.dynamic_slice_in_dim(
        shift_cols, (chip * 2 + core) * sequences, sequences, 0
    )
    condition_grad = lax.psum(jnp.dot(shift_mine, ada_weight_f.T, precision=PRECISE), "tensor")
    _, silu_back = jax.vjp(jax.nn.silu, time_emb.astype(f32))
    time_grad = silu_back(condition_grad)[0]

    text_half = text_size // 2
    text_rows = lax.dynamic_slice_in_dim(text_part, core * text_half, text_half, 0)
    text_away = lax.dynamic_slice_in_dim(text_part, (1 - core) * text_half, text_half, 0).astype(low)
    text_rows = (text_rows + swap_cores(text_away).astype(f32)).astype(low)
    text_pieces = []
    for turn in range(size):
        pairs = [
            (c * size + r, (r // 2) * size + (2 * (r % 2) + c + turn) % size)
            for c in range(2)
            for r in range(size)
        ]
        text_pieces.append(lax.ppermute(text_rows, ("core", "tensor"), pairs))
    text_stack = jnp.stack(text_pieces)
    text_grad = (
        jnp.stack([pick(text_stack, (rank - k) % size) for k in range(size)])
        .reshape(sequences, text_size, width)
        .astype(f32)
    )

    up_bias_rel = up_bias_part.reshape(chips, size, ff_part).transpose(1, 0, 2).reshape(size, ff_half)
    up_bias_abs = rolled(up_bias_rel, (size - rank) % size)
    up_bias_vec = jnp.stack(
        [jnp.where(core == 0, up_bias_abs, 0.0), jnp.where(core == 1, up_bias_abs, 0.0)], 1
    ).reshape(2 * size * ff_half)
    vectors = [
        skip_gain_part,
        skip_beta_part,
        skip_bias_part,
        self_gain_part,
        out_bias_part,
        gain2_part,
        beta2_part,
        cross_gain_part,
        cross_bias_part,
        gain3_part,
        beta3_part,
        up_bias_vec,
        down_bias_part,
    ]
    lengths = [vector.shape[0] for vector in vectors]
    summed = lax.psum(jnp.concatenate(vectors), ("chip", "core", "tensor"))
    sums = []
    at = 0
    for length in lengths:
        sums.append(summed[at : at + length])
        at += length

    def own_cols(vector, count):
        return lax.dynamic_slice_in_dim(vector, rank * count, count, 0)

    down0, down1 = reduce_rows(down_grad.reshape(chips, size, ff_part, width))
    down_weight_grad = jnp.concatenate(
        [down0.reshape(ff_half, width), down1.reshape(ff_half, width)], 0
    ).astype(f32)
    up0, up1 = reduce_rows(up_grad.reshape(chips, size, ff_part, width))
    up_weight_grad = jnp.concatenate(
        [up0.reshape(ff_half, width).T, up1.reshape(ff_half, width).T], 1
    ).astype(f32)
    cross0, cross1 = reduce_rows(cross_grads.reshape(4, size, half, width))

    def cols_of(first, second):
        return jnp.concatenate([first.T, second.T], 1).astype(f32)

    def rows_of(first, second):
        return jnp.concatenate([first, second], 0).astype(f32)

    cross_query_weight_grad = cols_of(cross0[0], cross1[0])
    cross_kv_weight_grad = jnp.stack([cols_of(cross0[i], cross1[i]) for i in (1, 2)])
    cross_out_weight_grad = rows_of(cross0[3], cross1[3])
    self0, self1 = reduce_rows(self_grads.reshape(4, size, half, width))
    qkv_weight_grad = jnp.stack([cols_of(self0[i], self1[i]) for i in range(3)])
    out_weight_grad = rows_of(self0[3], self1[3])
    skip_rel_grad = rolled(skip_sum.reshape(size, chips, skip_part, width), rank).transpose(1, 0, 2, 3)
    skip0, skip1 = reduce_rows(skip_rel_grad)
    skip_weight_grad = jnp.concatenate(
        [skip0.reshape(shard, width).T, skip1.reshape(shard, width).T], 0
    ).astype(f32)
    return (
        output_home,
        stats_home,
        latent_grad,
        skip_grad,
        text_grad,
        time_grad,
        sums[0],
        sums[1],
        skip_weight_grad,
        own_cols(sums[2], shard),
        ada_weight_grad,
        ada_bias_grad,
        qkv_weight_grad,
        sums[3].reshape(2, HD),
        out_weight_grad,
        sums[4],
        sums[5],
        sums[6],
        cross_query_weight_grad,
        cross_kv_weight_grad,
        sums[7].reshape(2, HD),
        cross_out_weight_grad,
        sums[8],
        sums[9],
        sums[10],
        up_weight_grad,
        own_cols(sums[11], 2 * ff_half),
        down_weight_grad,
        sums[12],
    )


def specs(dp):
    in_specs = (
        P(dp, "tensor", None),
        P(dp, "tensor", None),
        P(dp, None, None),
        P(dp),
        P(dp, None),
        P(dp, None, None),
        P(),
        P(),
        P(None, "tensor"),
        P("tensor"),
        P(None, "tensor"),
        P("tensor"),
        P(None, None, "tensor"),
        P(),
        P("tensor", None),
        P(),
        P(),
        P(),
        P(None, "tensor"),
        P(None, None, "tensor"),
        P(),
        P("tensor", None),
        P(),
        P(),
        P(),
        P(None, "tensor"),
        P("tensor"),
        P("tensor", None),
        P(),
        P(dp, "tensor", None),
    )
    out_specs = (
        P(dp, "tensor", None),
        P(dp, None, "tensor"),
        P(dp, "tensor", None),
        P(dp, "tensor", None),
        P(dp, None, None),
        P(dp, None),
        P(),
        P(),
        P(None, "tensor"),
        P("tensor"),
        P(None, "tensor"),
        P("tensor"),
        P(None, None, "tensor"),
        P(),
        P("tensor", None),
        P(),
        P(),
        P(),
        P(None, "tensor"),
        P(None, None, "tensor"),
        P(),
        P("tensor", None),
        P(),
        P(),
        P(),
        P(None, "tensor"),
        P("tensor"),
        P("tensor", None),
        P(),
    )
    return in_specs, out_specs


def solution(mesh):
    dp_size, size = mesh.shape["dp"], mesh.shape["tensor"]
    if dp_size == 8 and size == 4:
        grid = Mesh(mesh.devices.reshape(dp_size // 2, 2, size), ("chip", "core", "tensor"))
        in_specs, out_specs = specs(("chip", "core"))
        return jax.shard_map(
            chip_local, mesh=grid, in_specs=in_specs, out_specs=out_specs, check_vma=False
        )
    in_specs, out_specs = specs("dp")
    return jax.shard_map(
        tensor_local, mesh=mesh, in_specs=in_specs, out_specs=out_specs, check_vma=False
    )
```

```python
import functools
from functools import partial

import jax
import jax.numpy as jnp
from jax import lax
from jax.experimental import pallas as pl
from jax.experimental.pallas import tpu as pltpu
from jax.sharding import Mesh
from jax.sharding import PartitionSpec as P

HD = 88


EPSILON = 1e-06
ROPE_BASE = 10000.0
PRECISE = lax.Precision.HIGHEST


def layer_norm(values):
    center = values - jnp.mean(values, -1, keepdims=True)
    return center * lax.rsqrt(jnp.mean(center * center, -1, keepdims=True) + EPSILON)


def rope_tables(grid_pos):
    quarter = HD // 4
    frequency = ROPE_BASE ** (-jnp.arange(quarter, dtype=jnp.float32) / quarter)
    row_angle = grid_pos[..., 0:1].astype(jnp.float32) * frequency
    col_angle = grid_pos[..., 1:2].astype(jnp.float32) * frequency
    angles = jnp.concatenate([row_angle, row_angle, col_angle, col_angle], -1)
    return (jnp.cos(angles)[..., None, :], jnp.sin(angles)[..., None, :])


def rotate(values, cosines, sine_table):
    quarter = HD // 4
    first = values[..., :quarter]
    second = values[..., quarter : 2 * quarter]
    third = values[..., 2 * quarter : 3 * quarter]
    fourth = values[..., 3 * quarter :]
    turned = jnp.concatenate([-second, first, -fourth, third], -1)
    return values * cosines + turned * sine_table


def gather_tokens(values):
    return lax.all_gather(values, "tensor", axis=1, tiled=True)


def reduce_tokens(values):
    return lax.psum_scatter(
        values.astype(jnp.bfloat16), "tensor", scatter_dimension=1, tiled=True
    ).astype(jnp.float32)


def attend_forward(query_in, keys_in, values_in, key_bias):
    sequences, length, head_count, head_size = query_in.shape
    block_rows = min(512, length)
    query_blocks = jnp.moveaxis(
        query_in.reshape(sequences, length // block_rows, block_rows, head_count, head_size), 1, 0
    )

    def one_block(portion):
        scores = jnp.einsum(
            "sqhd,skhd->shqk", portion, keys_in, preferred_element_type=jnp.float32
        ) * HD ** (-0.5)
        scores = scores + key_bias[:, None, None, :]
        highest = jnp.max(scores, -1, keepdims=True)
        powers = jnp.exp(scores - highest)
        totals = jnp.sum(powers, -1, keepdims=True)
        weights = (powers / totals).astype(jnp.bfloat16)
        result = jnp.einsum(
            "shqk,skhd->sqhd", weights, values_in, preferred_element_type=jnp.float32
        )
        return (result, (highest + jnp.log(totals))[..., 0])

    results, logsum = lax.map(one_block, query_blocks)
    return (jnp.moveaxis(results, 0, 1).reshape(sequences, length, head_count * head_size), logsum)


def attend_backward(query_in, keys_in, values_in, key_bias, logsum, grad_mixed, result):
    sequences, length, head_count, head_size = query_in.shape
    block_rows = min(512, length)
    grad_heads = grad_mixed.reshape(sequences, length, head_count, head_size)
    delta = jnp.sum(
        grad_heads.astype(jnp.float32) * result.reshape(sequences, length, head_count, head_size),
        -1,
    )

    def cut_rows(array):
        return jnp.moveaxis(
            array.reshape((sequences, length // block_rows, block_rows) + array.shape[2:]), 1, 0
        )

    def one_block(running, item):
        keys_grad, values_grad = running
        portion, lse_part, grad_part, delta_part = item
        scores = jnp.einsum(
            "sqhd,skhd->shqk", portion, keys_in, preferred_element_type=jnp.float32
        ) * HD ** (-0.5)
        scores = scores + key_bias[:, None, None, :]
        weights = jnp.exp(scores - lse_part[..., None])
        values_grad = values_grad + jnp.einsum(
            "shqk,sqhd->skhd",
            weights.astype(jnp.bfloat16),
            grad_part,
            preferred_element_type=jnp.float32,
        )
        weight_grad = jnp.einsum(
            "sqhd,skhd->shqk", grad_part, values_in, preferred_element_type=jnp.float32
        )
        score_grad = (weights * (weight_grad - jnp.swapaxes(delta_part, 1, 2)[..., None])).astype(
            jnp.bfloat16
        )
        query_grad = jnp.einsum(
            "shqk,skhd->sqhd", score_grad, keys_in, preferred_element_type=jnp.float32
        ) * HD ** (-0.5)
        keys_grad = keys_grad + jnp.einsum(
            "shqk,sqhd->skhd", score_grad, portion, preferred_element_type=jnp.float32
        ) * HD ** (-0.5)
        return ((keys_grad, values_grad), query_grad)

    zero_keys = jnp.zeros(keys_in.shape, jnp.float32)
    (keys_grad, values_grad), query_grad = lax.scan(
        one_block,
        (zero_keys, zero_keys),
        (cut_rows(query_in), logsum, cut_rows(grad_heads), cut_rows(delta)),
    )
    query_grad = jnp.moveaxis(query_grad, 0, 1).reshape(query_in.shape)
    return (query_grad, keys_grad, values_grad)


def affine_norm(values, gain, beta):
    return layer_norm(values) * gain + beta


def tensor_local(
    latent_in,
    skip_in,
    text_emb,
    text_length,
    time_emb,
    grid_pos,
    skip_gain,
    skip_beta,
    skip_weight,
    skip_bias,
    ada_weight,
    ada_bias,
    query_key_value_weight,
    qk_gain,
    attention_output_weight,
    out_bias,
    norm2_gain,
    norm2_beta,
    crossed_query_weight,
    cross_kv_weight,
    cross_qk_gain,
    crossed_output_weight,
    cross_out_bias,
    norm3_gain,
    norm3_beta,
    up_projection_weight,
    up_bias,
    down_projection_weight,
    down_bias,
    out_grad,
):
    tensor_count = lax.axis_size("tensor")
    tensor_rank = lax.axis_index("tensor")
    sequences, local_len, model_width = latent_in.shape
    full_len = local_len * tensor_count
    col_width = ada_weight.shape[1]
    head_cols = query_key_value_weight.shape[2]
    local_heads = head_cols // HD
    cosines, sine_table = rope_tables(grid_pos)
    key_bias = jnp.where(
        jnp.arange(text_emb.shape[1])[None, :] < text_length[:, None], 0.0, -1e30
    ).astype(jnp.float32)
    self_bias = jnp.zeros((sequences, full_len), jnp.float32)
    skip_gain_f = skip_gain.astype(jnp.float32)
    skip_beta_f = skip_beta.astype(jnp.float32)
    norm2_gain_f = norm2_gain.astype(jnp.float32)
    norm2_beta_f = norm2_beta.astype(jnp.float32)
    norm3_gain_f = norm3_gain.astype(jnp.float32)
    norm3_beta_f = norm3_beta.astype(jnp.float32)
    qk_gain_f = qk_gain.astype(jnp.float32)
    cross_gain_f = cross_qk_gain.astype(jnp.float32)

    def first_norm(stream_in, shift_in):
        return layer_norm(stream_in) + shift_in[:, None, :]

    def qk_prep(raw, gain):
        return rotate(
            layer_norm(raw.reshape(sequences, full_len, local_heads, HD)) * gain,
            cosines,
            sine_table,
        )

    def head_norm(raw, gain):
        return layer_norm(raw.reshape(raw.shape[0], raw.shape[1], local_heads, HD)) * gain

    joined = jnp.concatenate([latent_in.astype(jnp.float32), skip_in.astype(jnp.float32)], -1)
    skip_normed = affine_norm(joined, skip_gain_f, skip_beta_f).astype(jnp.bfloat16)
    skip_all = gather_tokens(skip_normed)
    skip_cols = jnp.einsum(
        "slc,ce->sle", skip_all, skip_weight, preferred_element_type=jnp.float32
    ) + skip_bias.astype(jnp.float32)
    stream = lax.all_to_all(
        skip_cols.astype(jnp.bfloat16), "tensor", split_axis=1, concat_axis=2, tiled=True
    ).astype(skip_cols.dtype)
    condition = jax.nn.silu(time_emb.astype(jnp.float32))
    ada_weight_f = ada_weight.astype(jnp.float32)
    shift_part = jnp.dot(condition, ada_weight_f, precision=PRECISE) + ada_bias.astype(jnp.float32)
    shift_vec = lax.all_gather(shift_part, "tensor", axis=1, tiled=True)
    attn_in = first_norm(stream, shift_vec).astype(jnp.bfloat16)
    attention_gathered = gather_tokens(attn_in)
    projected = jnp.einsum(
        "mxp,jpc->jmxc",
        attention_gathered,
        query_key_value_weight,
        preferred_element_type=jnp.float32,
    )
    query_self = qk_prep(projected[0], qk_gain_f[0]).astype(jnp.bfloat16)
    keys_self = qk_prep(projected[1], qk_gain_f[1]).astype(jnp.bfloat16)
    values_self = projected[2].reshape(sequences, full_len, local_heads, HD).astype(jnp.bfloat16)
    attn_result, attn_logsum = attend_forward(query_self, keys_self, values_self, self_bias)
    attention_combined = attn_result.astype(jnp.bfloat16)
    branch_one = reduce_tokens(
        jnp.einsum(
            "jpe,ec->jpc",
            attention_combined,
            attention_output_weight,
            preferred_element_type=jnp.float32,
        )
    ) + out_bias.astype(jnp.float32)
    stream_two = stream + branch_one
    cross_in = affine_norm(stream_two, norm2_gain_f, norm2_beta_f).astype(jnp.bfloat16)
    crossed_gathered = gather_tokens(cross_in)
    query_raw = jnp.einsum(
        "pik,kx->pix", crossed_gathered, crossed_query_weight, preferred_element_type=jnp.float32
    )
    text_proj = jnp.einsum(
        "std,kdh->ksth", text_emb, cross_kv_weight, preferred_element_type=jnp.float32
    )
    cross_query = head_norm(query_raw, cross_gain_f[0]).astype(jnp.bfloat16)
    cross_keys = head_norm(text_proj[0], cross_gain_f[1]).astype(jnp.bfloat16)
    cross_values = (
        text_proj[1].reshape(sequences, text_proj.shape[2], local_heads, HD).astype(jnp.bfloat16)
    )
    cross_result, cross_logsum = attend_forward(cross_query, cross_keys, cross_values, key_bias)
    crossed_combined = cross_result.astype(jnp.bfloat16)
    branch_two = reduce_tokens(
        jnp.einsum(
            "jpe,ec->jpc",
            crossed_combined,
            crossed_output_weight,
            preferred_element_type=jnp.float32,
        )
    ) + cross_out_bias.astype(jnp.float32)
    stream_three = stream_two + branch_two
    mlp_in = affine_norm(stream_three, norm3_gain_f, norm3_beta_f).astype(jnp.bfloat16)
    gelu_fn = partial(jax.nn.gelu, approximate=True)
    perceptron_gathered = gather_tokens(mlp_in)
    hidden_pre = jnp.einsum(
        "ctk,kr->ctr", perceptron_gathered, up_projection_weight, preferred_element_type=jnp.float32
    ) + up_bias.astype(jnp.float32)
    hidden_state = gelu_fn(hidden_pre).astype(jnp.bfloat16)
    branch_three = reduce_tokens(
        jnp.einsum(
            "jgy,yv->jgv", hidden_state, down_projection_weight, preferred_element_type=jnp.float32
        )
    ) + down_bias.astype(jnp.float32)
    output = stream_three + branch_three
    stats = jnp.stack(
        [
            jnp.sqrt(jnp.mean(stream_term * stream_term, -1) + EPSILON)
            for stream_term in (stream, branch_one, branch_two, branch_three, output)
        ],
        1,
    )
    grad_out = out_grad.astype(jnp.float32)
    down_bias_part = jnp.sum(grad_out, axis=(0, 1))
    _, gelu_back = jax.vjp(gelu_fn, hidden_pre)
    gradient_gathered = gather_tokens(out_grad)
    hidden_grad = jnp.einsum(
        "bcq,eq->bce", gradient_gathered, down_projection_weight, preferred_element_type=jnp.float32
    )
    down_weight_grad = jnp.einsum(
        "mho,mhj->oj", hidden_state, gradient_gathered, preferred_element_type=jnp.float32
    )
    pre_grad = gelu_back(hidden_grad)[0]
    up_bias_grad = jnp.sum(pre_grad, axis=(0, 1))
    prenorm_reduced = pre_grad.astype(jnp.bfloat16)
    up_projection_gradient = jnp.einsum(
        "boy,bot->yt", perceptron_gathered, prenorm_reduced, preferred_element_type=jnp.float32
    )
    norm3_grad_in = reduce_tokens(
        jnp.einsum(
            "tke,ve->tkv", prenorm_reduced, up_projection_weight, preferred_element_type=jnp.float32
        )
    )
    _, norm3_back = jax.vjp(affine_norm, stream_three, norm3_gain_f, norm3_beta_f)
    from_three, gain3_part, beta3_part = norm3_back(norm3_grad_in)
    grad_three = grad_out + from_three
    cross_bias_part = jnp.sum(grad_three, axis=(0, 1))
    gradient_third_gathered = gather_tokens(grad_three.astype(jnp.bfloat16))
    cross_out_weight_grad = jnp.einsum(
        "kwy,kwn->yn", crossed_combined, gradient_third_gathered, preferred_element_type=jnp.float32
    )
    cross_mixed_grad = jnp.einsum(
        "ofz,iz->ofi",
        gradient_third_gathered,
        crossed_output_weight,
        preferred_element_type=jnp.float32,
    ).astype(jnp.bfloat16)
    cq_grad, ck_grad, cv_grad = attend_backward(
        cross_query,
        cross_keys,
        cross_values,
        key_bias,
        cross_logsum,
        cross_mixed_grad,
        cross_result,
    )
    _, cq_back = jax.vjp(head_norm, query_raw, cross_gain_f[0])
    query_raw_grad, cq_gain_part = cq_back(cq_grad)
    _, ck_back = jax.vjp(head_norm, text_proj[0], cross_gain_f[1])
    keys_raw_grad, ck_gain_part = ck_back(ck_grad)
    cross_gain_part = jnp.stack([cq_gain_part, ck_gain_part])
    query_reduced = query_raw_grad.astype(jnp.bfloat16)
    cross_query_weight_grad = jnp.einsum(
        "yfw,yfb->wb", crossed_gathered, query_reduced, preferred_element_type=jnp.float32
    )
    text_grads = jnp.stack(
        [keys_raw_grad, cv_grad.reshape(sequences, cv_grad.shape[1], head_cols)]
    ).astype(jnp.bfloat16)
    cross_kv_weight_grad = jnp.einsum(
        "std,ksth->kdh", text_emb, text_grads, preferred_element_type=jnp.float32
    )
    text_part = jnp.einsum(
        "ksth,kdh->std", text_grads, cross_kv_weight, preferred_element_type=jnp.float32
    )
    norm2_grad_in = reduce_tokens(
        jnp.einsum(
            "rjc,vc->rjv", query_reduced, crossed_query_weight, preferred_element_type=jnp.float32
        )
    )
    _, norm2_back = jax.vjp(affine_norm, stream_two, norm2_gain_f, norm2_beta_f)
    from_two, gain2_part, beta2_part = norm2_back(norm2_grad_in)
    grad_two = grad_three + from_two
    out_bias_part = jnp.sum(grad_two, axis=(0, 1))
    gradient_second_gathered = gather_tokens(grad_two.astype(jnp.bfloat16))
    out_weight_grad = jnp.einsum(
        "kwy,kwn->yn",
        attention_combined,
        gradient_second_gathered,
        preferred_element_type=jnp.float32,
    )
    attn_mixed_grad = jnp.einsum(
        "ofz,iz->ofi",
        gradient_second_gathered,
        attention_output_weight,
        preferred_element_type=jnp.float32,
    ).astype(jnp.bfloat16)
    sq_grad, sk_grad, sv_grad = attend_backward(
        query_self, keys_self, values_self, self_bias, attn_logsum, attn_mixed_grad, attn_result
    )
    _, sq_back = jax.vjp(qk_prep, projected[0], qk_gain_f[0])
    q_raw_grad, sq_gain_part = sq_back(sq_grad)
    _, sk_back = jax.vjp(qk_prep, projected[1], qk_gain_f[1])
    k_raw_grad, sk_gain_part = sk_back(sk_grad)
    self_gain_part = jnp.stack([sq_gain_part, sk_gain_part])
    projection_gradient = jnp.stack(
        [q_raw_grad, k_raw_grad, sv_grad.reshape(sequences, full_len, head_cols)]
    ).astype(jnp.bfloat16)
    qkv_weight_grad = jnp.einsum(
        "yze,myzi->mei", attention_gathered, projection_gradient, preferred_element_type=jnp.float32
    )
    first_grad_in = reduce_tokens(
        jnp.einsum(
            "apwf,acf->pwc",
            projection_gradient,
            query_key_value_weight,
            preferred_element_type=jnp.float32,
        )
    )
    _, first_back = jax.vjp(first_norm, stream, shift_vec)
    from_one, shift_part_grad = first_back(first_grad_in)
    grad_one = grad_two + from_one
    (
        shift_grad,
        down_bias_sum,
        gain3_sum,
        beta3_sum,
        cross_bias_sum,
        gain2_sum,
        beta2_sum,
        cross_gain_sum,
        out_bias_sum,
        self_gain_sum,
    ) = (
        lax.psum(shift_part_grad.astype(jnp.bfloat16), "tensor").astype(jnp.float32),
        lax.psum(down_bias_part.astype(jnp.bfloat16), "tensor").astype(jnp.float32),
        lax.psum(gain3_part.astype(jnp.bfloat16), "tensor").astype(jnp.float32),
        lax.psum(beta3_part.astype(jnp.bfloat16), "tensor").astype(jnp.float32),
        lax.psum(cross_bias_part.astype(jnp.bfloat16), "tensor").astype(jnp.float32),
        lax.psum(gain2_part.astype(jnp.bfloat16), "tensor").astype(jnp.float32),
        lax.psum(beta2_part.astype(jnp.bfloat16), "tensor").astype(jnp.float32),
        lax.psum(cross_gain_part.astype(jnp.bfloat16), "tensor").astype(jnp.float32),
        lax.psum(out_bias_part.astype(jnp.bfloat16), "tensor").astype(jnp.float32),
        lax.psum(self_gain_part.astype(jnp.bfloat16), "tensor").astype(jnp.float32),
    )
    shift_cols = lax.dynamic_slice_in_dim(shift_grad, tensor_rank * col_width, col_width, 1)
    ada_bias_grad = jnp.sum(shift_cols, axis=0)
    ada_weight_grad = jnp.dot(condition.T, shift_cols, precision=PRECISE)
    condition_grad = jnp.dot(shift_cols, ada_weight_f.T, precision=PRECISE)
    _, silu_back = jax.vjp(jax.nn.silu, time_emb.astype(jnp.float32))
    time_part = silu_back(condition_grad)[0]
    skip_grad_cols = lax.all_to_all(
        grad_one.astype(jnp.bfloat16), "tensor", split_axis=2, concat_axis=1, tiled=True
    ).astype(grad_one.dtype)
    skip_bias_grad = jnp.sum(skip_grad_cols, axis=(0, 1))
    skip_low = skip_grad_cols.astype(jnp.bfloat16)
    skip_weight_grad = jnp.einsum(
        "slc,sle->ce", skip_all, skip_low, preferred_element_type=jnp.float32
    )
    joined_grad_in = reduce_tokens(
        jnp.einsum("sle,ce->slc", skip_low, skip_weight, preferred_element_type=jnp.float32)
    )
    _, skip_norm_back = jax.vjp(affine_norm, joined, skip_gain_f, skip_beta_f)
    joined_grad, skip_gain_part, skip_beta_part = skip_norm_back(joined_grad_in)
    latent_grad = joined_grad[..., :model_width]
    skip_grad = joined_grad[..., model_width:]
    text_grad, time_grad, skip_gain_sum, skip_beta_sum = (
        lax.psum(text_part.astype(jnp.bfloat16), "tensor").astype(jnp.float32),
        lax.psum(time_part.astype(jnp.bfloat16), "tensor").astype(jnp.float32),
        lax.psum(skip_gain_part.astype(jnp.bfloat16), "tensor").astype(jnp.float32),
        lax.psum(skip_beta_part.astype(jnp.bfloat16), "tensor").astype(jnp.float32),
    )
    weight_sums = (
        lax.psum(skip_gain_sum.astype(jnp.bfloat16), "dp").astype(jnp.float32),
        lax.psum(skip_beta_sum.astype(jnp.bfloat16), "dp").astype(jnp.float32),
        lax.psum(skip_weight_grad.astype(jnp.bfloat16), "dp").astype(jnp.float32),
        lax.psum(skip_bias_grad.astype(jnp.bfloat16), "dp").astype(jnp.float32),
        lax.psum(ada_weight_grad.astype(jnp.bfloat16), "dp").astype(jnp.float32),
        lax.psum(ada_bias_grad.astype(jnp.bfloat16), "dp").astype(jnp.float32),
        lax.psum(qkv_weight_grad.astype(jnp.bfloat16), "dp").astype(jnp.float32),
        lax.psum(self_gain_sum.astype(jnp.bfloat16), "dp").astype(jnp.float32),
        lax.psum(out_weight_grad.astype(jnp.bfloat16), "dp").astype(jnp.float32),
        lax.psum(out_bias_sum.astype(jnp.bfloat16), "dp").astype(jnp.float32),
        lax.psum(gain2_sum.astype(jnp.bfloat16), "dp").astype(jnp.float32),
        lax.psum(beta2_sum.astype(jnp.bfloat16), "dp").astype(jnp.float32),
        lax.psum(cross_query_weight_grad.astype(jnp.bfloat16), "dp").astype(jnp.float32),
        lax.psum(cross_kv_weight_grad.astype(jnp.bfloat16), "dp").astype(jnp.float32),
        lax.psum(cross_gain_sum.astype(jnp.bfloat16), "dp").astype(jnp.float32),
        lax.psum(cross_out_weight_grad.astype(jnp.bfloat16), "dp").astype(jnp.float32),
        lax.psum(cross_bias_sum.astype(jnp.bfloat16), "dp").astype(jnp.float32),
        lax.psum(gain3_sum.astype(jnp.bfloat16), "dp").astype(jnp.float32),
        lax.psum(beta3_sum.astype(jnp.bfloat16), "dp").astype(jnp.float32),
        lax.psum(up_projection_gradient.astype(jnp.bfloat16), "dp").astype(jnp.float32),
        lax.psum(up_bias_grad.astype(jnp.bfloat16), "dp").astype(jnp.float32),
        lax.psum(down_weight_grad.astype(jnp.bfloat16), "dp").astype(jnp.float32),
        lax.psum(down_bias_sum.astype(jnp.bfloat16), "dp").astype(jnp.float32),
    )
    return (
        output.astype(jnp.bfloat16),
        stats,
        latent_grad,
        skip_grad,
        text_grad,
        time_grad,
    ) + tuple(weight_sums)


LANES = 128
LOG2E = 1.4426950408889634


def lane_index(shape):
    return lax.broadcasted_iota(jnp.int32, shape, 1)


def matmul_nt(left, right):
    return lax.dot_general(left, right, (((1,), (1,)), ((), ())), preferred_element_type=jnp.float32)


def matmul_nn(left, right):
    return lax.dot_general(left, right, (((1,), (0,)), ((), ())), preferred_element_type=jnp.float32)


def matmul_tn(left, right):
    return lax.dot_general(left, right, (((0,), (0,)), ((), ())), preferred_element_type=jnp.float32)


def row_sums(rows, both_parts=False):
    ones = jnp.ones((LANES, LANES), jnp.bfloat16)
    high = rows.astype(jnp.bfloat16)
    total = matmul_nn(high, ones)
    if both_parts:
        total = total + matmul_nn((rows - high.astype(jnp.float32)).astype(jnp.bfloat16), ones)
    return total


def norm_rows(raw):
    center = raw - row_sums(raw, True) * (1.0 / HD)
    center = jnp.where(lane_index(raw.shape) < HD, center, 0.0)
    inverse = lax.rsqrt(row_sums(center * center) * (1.0 / HD) + EPSILON)
    return center * inverse, inverse


def norm_rows_back(grad, normed, inverse):
    mean = row_sums(grad) * (1.0 / HD)
    along = row_sums(grad * normed) * (1.0 / HD)
    return jnp.where(lane_index(grad.shape) < HD, inverse * (grad - mean - normed * along), 0.0)


def turn_rows(rows, tables):
    quarter = HD // 4
    return (
        rows * tables[0]
        + pltpu.roll(rows, LANES - quarter, 1) * tables[1]
        + pltpu.roll(rows, quarter, 1) * tables[2]
    )


def turn_rows_back(grad, tables):
    quarter = HD // 4
    return (
        grad * tables[0]
        + pltpu.roll(grad * tables[1], quarter, 1)
        + pltpu.roll(grad * tables[2], LANES - quarter, 1)
    )


def kept_keys(count_ref, shape):
    return lax.broadcasted_iota(jnp.int32, shape, 0).astype(jnp.float32) < count_ref[0:1, :]


def attention_kernel(turned, rows, *refs):
    if turned:
        q_ref, k_ref, v_ref, gain_ref, count_ref, table_ref, out_ref, inv_ref = refs
    else:
        q_ref, k_ref, v_ref, gain_ref, count_ref, out_ref, inv_ref = refs
    low = jnp.bfloat16
    keys = norm_rows(k_ref[...])[0] * gain_ref[1:2, :]
    if turned:
        keys = turn_rows(keys, (table_ref[0], table_ref[1], table_ref[2]))
    values = v_ref[...]
    ones = jnp.ones(values.shape, jnp.float32)
    if not turned:
        kept = kept_keys(count_ref, values.shape)
        keys = jnp.where(kept, keys, 0.0)
        values = jnp.where(kept, values, 0.0)
        ones = jnp.where(kept, ones, 0.0)
    keys = keys.astype(low)
    mixed = jnp.concatenate([values.astype(low), ones.astype(low)], 1)
    for start in range(0, q_ref.shape[0], rows):
        part = pl.ds(start, rows)
        query = norm_rows(q_ref[part, :])[0] * gain_ref[0:1, :]
        if turned:
            query = turn_rows(query, tuple(table_ref[i, part, :] for i in range(3)))
        powers = jnp.exp2(matmul_nt(query.astype(low), keys)).astype(low)
        sums = matmul_nn(powers, mixed)
        inverse = 1.0 / sums[:, LANES:]
        out_ref[part, :] = (sums[:, :LANES] * inverse).astype(low)
        inv_ref[part, :] = inverse


def attention_back_kernel(turned, rows, *refs):
    if turned:
        q_ref, k_ref, v_ref, gain_ref, count_ref, table_ref = refs[:6]
        refs = refs[6:]
    else:
        q_ref, k_ref, v_ref, gain_ref, count_ref = refs[:5]
        refs = refs[5:]
    grad_ref, out_ref, inv_ref, dq_ref, dk_ref, dv_ref, dgain_ref, keys_acc, values_acc = refs
    low = jnp.bfloat16
    f32 = jnp.float32
    key_normed, key_inverse = norm_rows(k_ref[...])
    keys = key_normed * gain_ref[1:2, :]
    if turned:
        keys = turn_rows(keys, (table_ref[0], table_ref[1], table_ref[2]))
    else:
        kept = kept_keys(count_ref, keys.shape)
        keys = jnp.where(kept, keys, 0.0)
    keys = keys.astype(low)
    lane = lane_index(k_ref.shape)
    values = jnp.where((lane == HD) | (lane == HD + 1), 1.0, v_ref[...]).astype(low)
    factor = HD ** (-0.5)
    gain_total = jnp.zeros((1, LANES), f32)
    for start in range(0, q_ref.shape[0], rows):
        part = pl.ds(start, rows)
        query_normed, query_inverse = norm_rows(q_ref[part, :])
        query = query_normed * gain_ref[0:1, :]
        if turned:
            tables = tuple(table_ref[i, part, :] for i in range(3))
            query = turn_rows(query, tables)
        query = query.astype(low)
        grad = grad_ref[part, :].astype(f32) * inv_ref[part, :]
        delta = row_sums(grad * out_ref[part, :].astype(f32))
        delta_high = delta.astype(low).astype(f32)
        lane = lane_index((rows, LANES))
        grad_low = grad.astype(low)
        grad_more = jnp.where(
            lane == HD, -delta_high, jnp.where(lane == HD + 1, delta_high - delta, grad)
        ).astype(low)
        powers = jnp.exp2(matmul_nt(keys, query))
        score_grad = (powers * matmul_nt(values, grad_more)).astype(low)
        values_part = matmul_nn(powers.astype(low), grad_low)
        keys_part = matmul_nn(score_grad, query)
        if start == 0:
            values_acc[...] = values_part
            keys_acc[...] = keys_part
        else:
            values_acc[...] += values_part
            keys_acc[...] += keys_part
        query_grad = matmul_tn(score_grad, keys) * factor
        if turned:
            query_grad = turn_rows_back(query_grad, tables)
        gain_total = gain_total + jnp.sum(query_grad * query_normed, 0, keepdims=True)
        dq_ref[part, :] = norm_rows_back(
            query_grad * gain_ref[2:3, :], query_normed, query_inverse
        ).astype(low)
    values_grad = values_acc[...]
    key_grad = keys_acc[...] * (1.0 / LOG2E)
    if turned:
        key_grad = turn_rows_back(key_grad, (table_ref[0], table_ref[1], table_ref[2]))
    else:
        kept = kept_keys(count_ref, key_grad.shape)
        values_grad = jnp.where(kept, values_grad, 0.0)
        key_grad = jnp.where(kept, key_grad, 0.0)
    dv_ref[...] = values_grad.astype(low)
    dk_ref[...] = norm_rows_back(key_grad * gain_ref[1:2, :], key_normed, key_inverse).astype(low)
    dgain_ref[0, 0:1, :] = gain_total
    dgain_ref[0, 1:2, :] = jnp.sum(key_grad * key_normed, 0, keepdims=True)
    dgain_ref[0, 2:8, :] = jnp.zeros((6, LANES), f32)


def attention_specs(turned, length, key_length, q_at, k_at, v_at):
    specs = [
        pl.BlockSpec((length, LANES), lambda h: (0, q_at + h)),
        pl.BlockSpec((key_length, LANES), lambda h: (0, k_at + h)),
        pl.BlockSpec((key_length, LANES), lambda h: (0, v_at + h)),
        pl.BlockSpec((8, LANES), lambda h: (0, 0)),
        pl.BlockSpec((8, LANES), lambda h: (0, 0)),
    ]
    if turned:
        specs.append(pl.BlockSpec((3, length, LANES), lambda h: (0, 0, 0)))
    return specs


def attention(heads, query, keys, values, at, gains, count, tables=None, rows=256):
    length, key_length = query.shape[0], keys.shape[0]
    turned = tables is not None
    operands = [query, keys, values, gains, count] + ([tables] if turned else [])
    pairs = heads * length * key_length
    return pl.pallas_call(
        functools.partial(attention_kernel, turned, min(rows, length)),
        grid=(heads,),
        in_specs=attention_specs(turned, length, key_length, *at),
        out_specs=[
            pl.BlockSpec((length, LANES), lambda h: (0, h)),
            pl.BlockSpec((length, LANES), lambda h: (0, h)),
        ],
        out_shape=[
            jax.ShapeDtypeStruct((length, heads * LANES), jnp.bfloat16),
            jax.ShapeDtypeStruct((length, heads * LANES), jnp.float32),
        ],
        compiler_params=pltpu.CompilerParams(
            dimension_semantics=("arbitrary",), vmem_limit_bytes=40 * 2**20
        ),
        cost_estimate=pl.CostEstimate(
            flops=4 * pairs * LANES, transcendentals=pairs, bytes_accessed=18 * heads * length * LANES
        ),
        name="attention_turned" if turned else "attention_plain",
    )(*operands)


def attention_back(
    heads, query, keys, values, at, gains, count, grad, mixed, inverse, tables=None, rows=256
):
    length, key_length = query.shape[0], keys.shape[0]
    turned = tables is not None
    operands = [query, keys, values, gains, count] + ([tables] if turned else [])
    pairs = heads * length * key_length
    return pl.pallas_call(
        functools.partial(attention_back_kernel, turned, min(rows, length)),
        grid=(heads,),
        in_specs=attention_specs(turned, length, key_length, *at)
        + [pl.BlockSpec((length, LANES), lambda h: (0, h))] * 3,
        out_specs=[
            pl.BlockSpec((length, LANES), lambda h: (0, h)),
            pl.BlockSpec((key_length, LANES), lambda h: (0, h)),
            pl.BlockSpec((key_length, LANES), lambda h: (0, h)),
            pl.BlockSpec((1, 8, LANES), lambda h: (h, 0, 0)),
        ],
        out_shape=[
            jax.ShapeDtypeStruct((length, heads * LANES), jnp.bfloat16),
            jax.ShapeDtypeStruct((key_length, heads * LANES), jnp.bfloat16),
            jax.ShapeDtypeStruct((key_length, heads * LANES), jnp.bfloat16),
            jax.ShapeDtypeStruct((heads, 8, LANES), jnp.float32),
        ],
        scratch_shapes=[
            pltpu.VMEM((key_length, LANES), jnp.float32),
            pltpu.VMEM((key_length, LANES), jnp.float32),
        ],
        compiler_params=pltpu.CompilerParams(
            dimension_semantics=("arbitrary",), vmem_limit_bytes=40 * 2**20
        ),
        cost_estimate=pl.CostEstimate(
            flops=10 * pairs * LANES, transcendentals=pairs, bytes_accessed=30 * heads * length * LANES
        ),
        name="attention_turned_back" if turned else "attention_plain_back",
    )(*operands, grad, mixed, inverse)
def ring_pairs(size, step):
    return [(rank, (rank + step) % size) for rank in range(size)]


def swap_cores(values):
    return lax.ppermute(values, "core", [(0, 1), (1, 0)])


def from_later(values, step, size):
    return lax.ppermute(values, "tensor", ring_pairs(size, -step))


def from_earlier(values, step, size):
    return lax.ppermute(values, "tensor", ring_pairs(size, step))


def spread_pairs(size, turn):
    pairs = []
    for core in range(2):
        for rank in range(size):
            piece = (rank + turn) % size
            pairs.append((core * size + rank, (piece % 2) * size + 2 * core + piece // 2))
    return pairs


def pick(array, index):
    return lax.dynamic_index_in_dim(array, index, 0, keepdims=False)


def rolled(array, start):
    return lax.dynamic_slice_in_dim(jnp.concatenate([array, array], 0), start, array.shape[0], 0)


def tie(*values):
    return lax.optimization_barrier(values)


def dot_tt(left, right):
    return lax.dot_general(left, right, (((1,), (1,)), ((), ())), preferred_element_type=jnp.float32)


def dot_nn(left, right):
    return lax.dot_general(left, right, (((1,), (0,)), ((), ())), preferred_element_type=jnp.float32)


def dot_tn(left, right):
    return lax.dot_general(left, right, (((0,), (0,)), ((), ())), preferred_element_type=jnp.float32)


def chip_local(
    latent_in,
    skip_in,
    text_emb,
    text_length,
    time_emb,
    grid_pos,
    skip_gain,
    skip_beta,
    skip_weight,
    skip_bias,
    ada_weight,
    ada_bias,
    query_key_value_weight,
    qk_gain,
    attention_output_weight,
    out_bias,
    norm2_gain,
    norm2_beta,
    crossed_query_weight,
    cross_kv_weight,
    cross_qk_gain,
    crossed_output_weight,
    cross_out_bias,
    norm3_gain,
    norm3_beta,
    up_projection_weight,
    up_bias,
    down_projection_weight,
    down_bias,
    out_grad,
):
    f32 = jnp.float32
    low = jnp.bfloat16
    size = lax.axis_size("tensor")
    chips = lax.axis_size("chip")
    rank = lax.axis_index("tensor")
    core = lax.axis_index("core")
    chip = lax.axis_index("chip")
    sequences, local_len, width = latent_in.shape
    piece_len = local_len // 2
    own_len = size * piece_len
    shard = ada_weight.shape[1]
    half = shard // 2
    heads = size * half // HD
    ff_half = up_bias.shape[0] // 2
    ff_part = ff_half // chips
    lanes = heads * LANES
    at_home = core == rank // sequences

    def spread(values):
        return jnp.stack(
            [
                lax.ppermute(
                    pick(values, (rank + turn) % size), ("core", "tensor"), spread_pairs(size, turn)
                )
                for turn in range(size)
            ]
        )

    def collect(values):
        parts = [
            lax.ppermute(
                values[turn],
                ("core", "tensor"),
                [(target, source) for source, target in spread_pairs(size, turn)],
            )
            for turn in range(size)
        ]
        return rolled(jnp.stack(parts), (size - rank) % size)

    def of_sequence(values):
        mine = pick(values, rank % sequences)
        return jnp.where(at_home, mine, swap_cores(mine))

    def both(values):
        return jnp.concatenate([values, swap_cores(values)], 0)

    def halve(values):
        return values[:own_len] + swap_cores(values[own_len:].astype(low)).astype(f32)

    def quarters(owns):
        mine = jnp.concatenate([pick(own, chip) for own in owns], 0)
        later = jnp.stack([from_later(mine, step, size) for step in range(1, size)])
        parts, at = [], 0
        for own in owns:
            parts.append(later[:, at : at + own.shape[1]])
            at += own.shape[1]
        return parts

    def gather_shares(later):
        return lax.all_gather(later, "chip", axis=0, tiled=False)

    def gather_rows(own, later):
        return jnp.concatenate([own[:, None], gather_shares(later)], 1)

    def pad_heads(own, rest):
        own = own.reshape(own.shape[0], 1, half // HD, HD, width)
        rest = rest.reshape(own.shape[0], size - 1, half // HD, HD, width)
        zero = jnp.zeros((), low)
        nothing = (0, 0, 0)
        own = lax.pad(own, zero, (nothing, (0, size - 1, 0), nothing, (0, LANES - HD, 0), nothing))
        rest = lax.pad(rest, zero, (nothing, (1, 0, 0), nothing, (0, LANES - HD, 0), nothing))
        return (own + rest).reshape(-1, lanes, width)

    def trim_heads(rows):
        return rows.reshape(heads, LANES, width)[:, :HD].reshape(size, half, width)

    def by_core(own):
        other = swap_cores(own)
        return jnp.where(core == 0, own, other), jnp.where(core == 0, other, own)

    def scatter_rows(partial_sums):
        rows = partial_sums.shape[2]
        return lax.psum_scatter(
            partial_sums.reshape(chips * size * rows, width), "chip", scatter_dimension=0, tiled=True
        ).reshape(size, rows, width)

    def send_line(parts):
        return [from_earlier(parts[step], step, size) for step in range(1, size)]

    def add_line(own, arrived):
        total = own.astype(f32)
        for part in arrived:
            total = total + part.astype(f32)
        return total.astype(low)

    def share_rows(total):
        return lax.all_gather(total, "chip", axis=0, tiled=True)

    def half_cols(weight):
        return lax.dynamic_slice_in_dim(weight, core * half, half, 1).T

    def half_rows(weight):
        return lax.dynamic_slice_in_dim(weight, core * half, half, 0)

    skip_half = lax.dynamic_slice_in_dim(skip_weight, core * width, width, 0).T
    skip_part = shard // chips
    (skip_later,) = quarters([skip_half.reshape(chips, skip_part, width)])
    skip_mine = pick(skip_half.reshape(chips, skip_part, width), chip)
    skip_abs = rolled(jnp.concatenate([skip_mine[None], skip_later], 0), (size - rank) % size)
    skip_own_w = gather_shares(skip_abs).transpose(1, 0, 2, 3).reshape(width, width)

    self_own = jnp.stack(
        [half_cols(query_key_value_weight[i]) for i in range(3)]
        + [half_rows(attention_output_weight)]
    )
    cross_own = jnp.stack(
        [half_cols(crossed_query_weight), half_cols(cross_kv_weight[0]), half_cols(cross_kv_weight[1])]
        + [half_rows(crossed_output_weight)]
    )
    up_own = lax.dynamic_slice_in_dim(up_projection_weight, core * ff_half, ff_half, 1).T
    up_own = up_own.reshape(chips, ff_part, width)
    down_own = lax.dynamic_slice_in_dim(down_projection_weight, core * ff_half, ff_half, 0)
    down_own = down_own.reshape(chips, ff_part, width)
    skip_other_w = swap_cores(skip_own_w)
    condition = jax.nn.silu(time_emb.astype(f32))
    ada_weight_f = ada_weight.astype(f32)
    shift_part = jnp.dot(condition, ada_weight_f, precision=PRECISE) + ada_bias.astype(f32)
    shift_part = shift_part.reshape(sequences * shard)
    shift_high = shift_part.astype(low)
    shift_low = (shift_part - shift_high.astype(f32)).astype(low)
    up_bias_own = lax.dynamic_slice_in_dim(up_bias, core * ff_half, ff_half, 0)
    small = jnp.concatenate([shift_high, shift_low, skip_bias, up_bias_own])
    small_size = small.shape[0]
    small_rows = 8 * -(-small_size // (8 * width))
    small = jnp.pad(small, (0, small_rows * width - small_size)).reshape(1, small_rows, width)
    small = jnp.broadcast_to(small, (chips, small_rows, width))
    self_later, small_later = quarters([self_own, small])
    (cross_later,) = quarters([cross_own])
    up_later, down_later = quarters([up_own, down_own])
    self_full = pad_heads(self_own, gather_shares(self_later))
    cross_full = pad_heads(cross_own, gather_shares(cross_later))

    small_rel = jnp.concatenate([small[:1], small_later], 0).reshape(size, -1)[:, :small_size].astype(f32)
    shift_size = sequences * shard
    up_bias_f = (
        small_rel[:, 2 * shift_size + shard :]
        .reshape(size, chips, ff_part)
        .transpose(1, 0, 2)
        .reshape(size * ff_half)
    )
    small_rel = jnp.concatenate(
        [
            small_rel[:, :shift_size] + small_rel[:, shift_size : 2 * shift_size],
            small_rel[:, 2 * shift_size : 2 * shift_size + shard],
        ],
        1,
    )
    small_abs = rolled(small_rel, (size - rank) % size)
    small_abs = small_abs.reshape(size, sequences + 1, shard).transpose(1, 0, 2)
    small_abs = small_abs.reshape(sequences + 1, width)
    skip_bias_f = small_abs[sequences]
    full_len = grid_pos.shape[1]
    of_mine = of_sequence(
        jnp.concatenate(
            [
                small_abs[:sequences],
                text_length.astype(f32)[:, None],
                grid_pos.astype(f32).transpose(0, 2, 1).reshape(sequences, 2 * full_len),
            ],
            1,
        )
    )
    shift_vec = of_mine[:width]
    key_count = jnp.broadcast_to(of_mine[width], (8, LANES))
    positions = of_mine[width + 1 :].reshape(2, 2 * size, piece_len)
    text_own = of_sequence(text_emb)
    text_size = text_own.shape[0]

    by_piece = positions.transpose(1, 0, 2)

    def piece_index(of_core, turn):
        source = (2 * (rank % 2) + of_core - turn) % size
        return source * 2 + of_core

    ordered = jnp.concatenate(
        [pick(by_piece, piece_index(of_core, turn)) for of_core in (core, 1 - core) for turn in range(size)],
        1,
    )
    lane = jnp.arange(LANES)
    quarter = lane // (HD // 4)
    frequency = ROPE_BASE ** (-(lane % (HD // 4)).astype(f32) / (HD // 4))
    angles = ordered[0][:, None] * jnp.where(quarter < 2, frequency, 0.0)[None, :]
    angles = angles + ordered[1][:, None] * jnp.where(quarter < 2, 0.0, frequency)[None, :]
    real_lane = lane < HD
    sines = jnp.sin(angles)
    tables = jnp.stack(
        [
            jnp.where(real_lane, jnp.cos(angles), 0.0),
            jnp.where(real_lane & (quarter % 2 == 0), -sines, 0.0),
            jnp.where(real_lane & (quarter % 2 == 1), sines, 0.0),
        ]
    )

    def kernel_gains(gains):
        rows = jnp.stack([gains[0] * (HD ** (-0.5) * LOG2E), gains[1], gains[0]])
        return jnp.pad(rows, ((0, 5), (0, LANES - HD)))

    skip_gain_f = skip_gain.astype(f32)
    skip_beta_f = skip_beta.astype(f32)
    norm2_gain_f = norm2_gain.astype(f32)
    norm2_beta_f = norm2_beta.astype(f32)
    norm3_gain_f = norm3_gain.astype(f32)
    norm3_beta_f = norm3_beta.astype(f32)

    def first_norm(stream_in, shift_in):
        return layer_norm(stream_in) + shift_in[None, :]

    self_gains = kernel_gains(qk_gain.astype(f32))
    cross_gains = kernel_gains(cross_qk_gain.astype(f32))

    latent_f = latent_in.reshape(own_len, width).astype(f32)
    skip_f = skip_in.reshape(own_len, width).astype(f32)
    joined_size = 2 * width
    center = (jnp.sum(latent_f, -1, keepdims=True) + jnp.sum(skip_f, -1, keepdims=True)) / joined_size
    latent_c = latent_f - center
    skip_c = skip_f - center
    spread_sq = jnp.sum(latent_c * latent_c, -1, keepdims=True) + jnp.sum(
        skip_c * skip_c, -1, keepdims=True
    )
    inverse = lax.rsqrt(spread_sq / joined_size + EPSILON)
    normed = jnp.stack(
        [
            (latent_c * inverse * skip_gain_f[:width] + skip_beta_f[:width]).astype(low),
            (skip_c * inverse * skip_gain_f[width:] + skip_beta_f[width:]).astype(low),
        ]
    )
    normed_own = pick(normed, core)
    normed_other = pick(normed, 1 - core)
    stream_home = (
        dot_tt(normed_own, skip_own_w) + dot_tt(normed_other, skip_other_w) + skip_bias_f
    ).astype(low)
    stream_low = spread(stream_home.reshape(size, piece_len, width)).reshape(own_len, width)
    stream = stream_low.astype(f32)

    attn_in = both(first_norm(stream, shift_vec).astype(low))
    projected = dot_tt(attn_in, self_full[:3].reshape(3 * lanes, width))
    projected, grad_home = tie(projected, out_grad)
    grad_low = spread(grad_home.reshape(size, piece_len, width)).reshape(own_len, width)
    self_inputs = (heads, projected, projected, projected, (0, heads, 2 * heads), self_gains, key_count)
    attention_combined, self_inverse = attention(*self_inputs, tables, rows=2 * own_len)
    up_full = gather_rows(up_own, up_later).reshape(size * ff_half, width)
    down_full = gather_rows(down_own, down_later).reshape(size * ff_half, width)
    branch_one = halve(dot_nn(attention_combined, self_full[3])) + out_bias.astype(f32)
    stream_two = stream + branch_one
    cross_in = both(affine_norm(stream_two, norm2_gain_f, norm2_beta_f).astype(low))
    query_raw = dot_tt(cross_in, cross_full[0])
    text_raw = dot_tt(text_own, cross_full[1:3].reshape(2 * lanes, width))
    cross_inputs = (heads, query_raw, text_raw, text_raw, (0, 0, heads), cross_gains, key_count)
    crossed_combined, cross_inverse = attention(*cross_inputs, rows=2 * own_len)
    branch_two = halve(dot_nn(crossed_combined, cross_full[3])) + cross_out_bias.astype(f32)
    stream_three = stream_two + branch_two
    mlp_in = both(affine_norm(stream_three, norm3_gain_f, norm3_beta_f).astype(low))
    gelu_fn = partial(jax.nn.gelu, approximate=True)
    hidden_pre = dot_tt(mlp_in, up_full) + up_bias_f
    hidden_state, gelu_back = jax.vjp(gelu_fn, hidden_pre)
    hidden_state = hidden_state.astype(low)
    branch_three = halve(dot_nn(hidden_state, down_full)) + down_bias.astype(f32)
    output = stream_three + branch_three
    stats = jnp.stack(
        [
            jnp.sqrt(jnp.mean(term * term, -1) + EPSILON)
            for term in (stream, branch_one, branch_two, branch_three, output)
        ]
    )
    stat_rows = stats.reshape(5, size, piece_len).transpose(1, 0, 2).reshape(size, 1, 5 * piece_len)
    stat_rows = jnp.pad(stat_rows.astype(low), ((0, 0), (0, 7), (0, width - 5 * piece_len)))
    home = collect(jnp.concatenate([output.astype(low).reshape(size, piece_len, width), stat_rows], 1))
    output_home = home[:, :piece_len].reshape(latent_in.shape)
    stats_home = (
        home[:, piece_len, : 5 * piece_len]
        .reshape(sequences, 2, 5, piece_len)
        .transpose(0, 2, 1, 3)
        .reshape(sequences, 5, local_len)
        .astype(f32)
    )

    grad_out = grad_low.astype(f32)
    down_bias_part = jnp.sum(grad_out, axis=0)
    grad_all = both(grad_low)
    down_grad = dot_tn(hidden_state, grad_all).astype(low)
    grad_all, down_grad = tie(grad_all, down_grad)
    down_parts = scatter_rows(down_grad.reshape(chips, size, ff_part, width))
    hidden_grad = dot_tt(grad_all, down_full)
    pre_grad = gelu_back(hidden_grad)[0]
    up_bias_part = jnp.sum(pre_grad, axis=0)
    pre_low = pre_grad.astype(low)
    up_grad = dot_tn(pre_low, mlp_in).astype(low)
    pre_low, up_grad = tie(pre_low, up_grad)
    up_parts = scatter_rows(up_grad.reshape(chips, size, ff_part, width))
    norm3_grad_in = halve(dot_nn(pre_low, up_full))
    _, norm3_back = jax.vjp(affine_norm, stream_three, norm3_gain_f, norm3_beta_f)
    from_three, gain3_part, beta3_part = norm3_back(norm3_grad_in)
    grad_three = grad_out + from_three
    cross_bias_part = jnp.sum(grad_three, axis=0)
    three_all = both(grad_three.astype(low))
    cross_out_grad = dot_tn(crossed_combined, three_all)
    cross_mixed_grad = dot_tt(three_all, cross_full[3]).astype(low)
    query_low, keys_low, values_low, cross_gain_sums = attention_back(
        *cross_inputs, cross_mixed_grad, crossed_combined, cross_inverse, rows=2 * own_len
    )
    norm2_grad_in = halve(dot_nn(query_low, cross_full[0]))
    cross_grads = jnp.stack(
        [
            trim_heads(grad.astype(low))
            for grad in (
                dot_tn(query_low, cross_in),
                dot_tn(keys_low, text_own),
                dot_tn(values_low, text_own),
                cross_out_grad,
            )
        ],
    )
    cross_parts = scatter_rows(cross_grads)
    text_part = dot_nn(keys_low, cross_full[1]) + dot_nn(values_low, cross_full[2])
    _, norm2_back = jax.vjp(affine_norm, stream_two, norm2_gain_f, norm2_beta_f)
    from_two, gain2_part, beta2_part = norm2_back(norm2_grad_in)
    grad_two = grad_three + from_two
    out_bias_part = jnp.sum(grad_two, axis=0)
    two_all = both(grad_two.astype(low))
    out_weight_part = dot_tn(attention_combined, two_all)
    attn_mixed_grad = dot_tt(two_all, self_full[3]).astype(low)
    *proj_grads, self_gain_sums = attention_back(
        *self_inputs, attn_mixed_grad, attention_combined, self_inverse, tables, rows=2 * own_len
    )
    first_grad_in = halve(
        dot_nn(proj_grads[0], self_full[0])
        + dot_nn(proj_grads[1], self_full[1])
        + dot_nn(proj_grads[2], self_full[2])
    )
    self_grads = jnp.stack(
        [trim_heads(dot_tn(grad, attn_in).astype(low)) for grad in proj_grads]
        + [trim_heads(out_weight_part.astype(low))],
    )
    _, first_back = jax.vjp(first_norm, stream, shift_vec)
    from_one, shift_own_grad = first_back(first_grad_in)
    grad_one = (grad_two + from_one).astype(low)
    down_sum = share_rows(add_line(down_parts[0], send_line(down_parts)))
    up_sum = share_rows(add_line(up_parts[0], send_line(up_parts)))
    grad_one, self_grads = tie(grad_one, self_grads)
    self_parts = scatter_rows(self_grads)

    home_grad = collect(grad_one.reshape(size, piece_len, width)).reshape(own_len, width)
    skip_bias_part = jnp.sum(home_grad.astype(f32), axis=0)
    skip_own_grad = dot_tn(home_grad, normed_own)
    skip_other_grad = dot_tn(home_grad, normed_other).astype(low)
    skip_sum = (skip_own_grad + swap_cores(skip_other_grad).astype(f32)).astype(low)
    own_in = dot_nn(home_grad, skip_own_w)
    other_in = dot_nn(home_grad, skip_other_w)
    latent_in_grad = jnp.where(core == 0, own_in, other_in)
    skip_in_grad = jnp.where(core == 0, other_in, own_in)
    latent_ln = latent_c * inverse
    skip_ln = skip_c * inverse
    skip_gain_part = jnp.concatenate(
        [jnp.sum(latent_in_grad * latent_ln, 0), jnp.sum(skip_in_grad * skip_ln, 0)]
    )
    skip_beta_part = jnp.concatenate([jnp.sum(latent_in_grad, 0), jnp.sum(skip_in_grad, 0)])
    latent_h = latent_in_grad * skip_gain_f[:width]
    skip_h = skip_in_grad * skip_gain_f[width:]
    mean_h = (jnp.sum(latent_h, -1, keepdims=True) + jnp.sum(skip_h, -1, keepdims=True)) / joined_size
    mean_hl = (
        jnp.sum(latent_h * latent_ln, -1, keepdims=True)
        + jnp.sum(skip_h * skip_ln, -1, keepdims=True)
    ) / joined_size
    latent_grad = (inverse * (latent_h - mean_h - latent_ln * mean_hl)).reshape(latent_in.shape)
    skip_grad = (inverse * (skip_h - mean_h - skip_ln * mean_hl)).reshape(latent_in.shape)

    shift_own = shift_own_grad + swap_cores(shift_own_grad)
    shift_line = rolled(
        jnp.stack([shift_own] + [from_later(shift_own, step, size) for step in range(1, size)]),
        (size - rank) % size,
    )
    line_cols = lax.dynamic_slice_in_dim(shift_line, rank * shard, shard, 1)
    condition_part = jnp.dot(line_cols, ada_weight_f.T, precision=PRECISE)

    text_half = text_size // 2
    text_rows = lax.dynamic_slice_in_dim(text_part, core * text_half, text_half, 0)
    text_away = lax.dynamic_slice_in_dim(text_part, (1 - core) * text_half, text_half, 0).astype(low)
    text_rows = (text_rows + swap_cores(text_away).astype(f32)).astype(low)
    text_pieces = []
    for turn in range(size):
        pairs = [
            (c * size + r, (r // 2) * size + (2 * (r % 2) + c + turn) % size)
            for c in range(2)
            for r in range(size)
        ]
        text_pieces.append(lax.ppermute(text_rows, ("core", "tensor"), pairs))
    text_stack = jnp.stack(text_pieces)
    text_grad = (
        jnp.stack([pick(text_stack, (rank - k) % size) for k in range(size)])
        .reshape(sequences, text_size, width)
        .astype(f32)
    )

    up_bias_rel = up_bias_part.reshape(chips, size, ff_part).transpose(1, 0, 2).reshape(size, ff_half)
    up_bias_abs = rolled(up_bias_rel, (size - rank) % size)
    up_bias_vec = jnp.stack(
        [jnp.where(core == 0, up_bias_abs, 0.0), jnp.where(core == 1, up_bias_abs, 0.0)], 1
    ).reshape(2 * size * ff_half)
    gain_rows = jnp.concatenate(
        [jnp.sum(sums[:, :2], 0)[:, :HD].reshape(2 * HD) for sums in (self_gain_sums, cross_gain_sums)]
    )
    last_row = 2 * size * ff_half % width
    vector_rows = jnp.concatenate(
        [
            skip_gain_part,
            skip_beta_part,
            skip_bias_part,
            out_bias_part,
            gain2_part,
            beta2_part,
            cross_bias_part,
            gain3_part,
            beta3_part,
            down_bias_part,
            up_bias_vec,
            gain_rows,
            jnp.zeros((width - last_row - gain_rows.shape[0],), f32),
        ]
    ).reshape(-1, width)
    first_core = core == 0
    line_rows = jnp.stack(
        [
            jnp.where(first_core, condition_part, 0.0),
            jnp.where(first_core & (rank == 0), shift_line, 0.0),
        ]
    )
    chip_rows = jnp.where(
        (jnp.arange(chips) == chip)[None, :, None, None], line_rows[:, None], 0.0
    ).reshape(2 * chips * size, width)
    time_rows = jnp.where(
        (jnp.arange(2 * chips) == 2 * chip + core)[:, None, None] & (rank == 0),
        time_emb.astype(f32)[None],
        0.0,
    ).reshape(2 * chips * sequences, width)
    vectors = jnp.concatenate([chip_rows, time_rows, vector_rows], 0)
    vector_part = 32 * -(-vectors.shape[0] // (32 * chips))
    vectors = jnp.pad(vectors, ((0, chips * vector_part - vectors.shape[0]), (0, 0)))
    vectors = vectors.astype(low).reshape(chips, vector_part, width)

    def own_cols(vector, count):
        return lax.dynamic_slice_in_dim(vector, rank * count, count, 0)

    skip_rel_grad = rolled(skip_sum.reshape(size, chips, skip_part, width), rank).transpose(1, 0, 2, 3)
    skip_rows = size * skip_part
    skip_rows_all = jnp.concatenate([skip_rel_grad.reshape(chips, skip_rows, width), vectors], 1)
    skip_rows_all, self_parts, down_sum, up_sum = tie(skip_rows_all, self_parts, down_sum, up_sum)
    parts = lax.psum_scatter(
        skip_rows_all.reshape(-1, width), "chip", scatter_dimension=0, tiled=True
    )
    cross_sum, self_sum = (
        share_rows(add_line(parts[0], send_line(parts))) for parts in (cross_parts, self_parts)
    )
    down0, down1 = by_core(down_sum)
    down_weight_grad = jnp.concatenate([down0, down1], 0).astype(f32)
    up0, up1 = by_core(up_sum)
    up_weight_grad = jnp.concatenate([up0.T, up1.T], 1).astype(f32)
    cross0, cross1 = (part.reshape(4, half, width) for part in by_core(cross_sum))

    def cols_of(first, second):
        return jnp.concatenate([first.T, second.T], 1).astype(f32)

    def rows_of(first, second):
        return jnp.concatenate([first, second], 0).astype(f32)

    cross_query_weight_grad = cols_of(cross0[0], cross1[0])
    cross_kv_weight_grad = jnp.stack([cols_of(cross0[i], cross1[i]) for i in (1, 2)])
    cross_out_weight_grad = rows_of(cross0[3], cross1[3])
    self0, self1 = (part.reshape(4, half, width) for part in by_core(self_sum))
    qkv_weight_grad = jnp.stack([cols_of(self0[i], self1[i]) for i in range(3)])
    out_weight_grad = rows_of(self0[3], self1[3])
    vector_mine = parts[skip_rows:]
    skip_total = parts[:skip_part].astype(f32)
    vector_line = [vector_mine]
    for step in range(1, size):
        arrived = from_earlier(
            jnp.concatenate([parts[step * skip_part : (step + 1) * skip_part], vector_mine], 0), step, size
        )
        skip_total = skip_total + arrived[:skip_part].astype(f32)
        vector_line.append(arrived[skip_part:])
    vector_line = jnp.stack(vector_line)
    vector_total = pick(vector_line, rank).astype(f32)
    for source in range(1, size):
        vector_total = vector_total + pick(vector_line, (rank - source) % size).astype(f32)
    total = lax.all_gather(
        jnp.concatenate([skip_total, vector_total], 0).astype(low), "chip", axis=0, tiled=True
    ).reshape(chips, skip_part + vector_part, width)
    total_other = swap_cores(total)
    skip0 = jnp.where(core == 0, total[:, :skip_part], total_other[:, :skip_part])
    skip1 = jnp.where(core == 0, total_other[:, :skip_part], total[:, :skip_part])
    skip_weight_grad = jnp.concatenate(
        [skip0.reshape(shard, width).T, skip1.reshape(shard, width).T], 0
    ).astype(f32)
    summed = (total[:, skip_part:].astype(f32) + total_other[:, skip_part:].astype(f32)).reshape(-1, width)
    seqs = chips * size
    own_seq = (chip * 2 + core) * sequences
    time_back = lax.dynamic_slice_in_dim(summed[:seqs], own_seq, sequences, 0)
    _, silu_back = jax.vjp(jax.nn.silu, time_emb.astype(f32))
    time_grad = silu_back(time_back)[0]
    shift_cols = lax.dynamic_slice_in_dim(summed[seqs : 2 * seqs], rank * shard, shard, 1)
    condition_all = jax.nn.silu(summed[2 * seqs : 3 * seqs])
    ada_bias_grad = jnp.sum(shift_cols, axis=0)
    ada_weight_grad = jnp.dot(condition_all.T, shift_cols, precision=PRECISE)
    flat = summed[3 * seqs :].reshape(-1)
    rows_at = [flat[width * i : width * (i + 1)] for i in range(12)]
    up_bias_sum = flat[12 * width : 12 * width + 2 * size * ff_half]
    gain_sums = flat[12 * width + 2 * size * ff_half :][: 4 * HD].reshape(2, 2, HD)
    return (
        output_home,
        stats_home,
        latent_grad,
        skip_grad,
        text_grad,
        time_grad,
        flat[: 2 * width],
        flat[2 * width : 4 * width],
        skip_weight_grad,
        own_cols(rows_at[4], shard),
        ada_weight_grad,
        ada_bias_grad,
        qkv_weight_grad,
        gain_sums[0],
        out_weight_grad,
        rows_at[5],
        rows_at[6],
        rows_at[7],
        cross_query_weight_grad,
        cross_kv_weight_grad,
        gain_sums[1],
        cross_out_weight_grad,
        rows_at[8],
        rows_at[9],
        rows_at[10],
        up_weight_grad,
        own_cols(up_bias_sum, 2 * ff_half),
        down_weight_grad,
        rows_at[11],
    )


def specs(dp):
    in_specs = (
        P(dp, "tensor", None),
        P(dp, "tensor", None),
        P(dp, None, None),
        P(dp),
        P(dp, None),
        P(dp, None, None),
        P(),
        P(),
        P(None, "tensor"),
        P("tensor"),
        P(None, "tensor"),
        P("tensor"),
        P(None, None, "tensor"),
        P(),
        P("tensor", None),
        P(),
        P(),
        P(),
        P(None, "tensor"),
        P(None, None, "tensor"),
        P(),
        P("tensor", None),
        P(),
        P(),
        P(),
        P(None, "tensor"),
        P("tensor"),
        P("tensor", None),
        P(),
        P(dp, "tensor", None),
    )
    out_specs = (
        P(dp, "tensor", None),
        P(dp, None, "tensor"),
        P(dp, "tensor", None),
        P(dp, "tensor", None),
        P(dp, None, None),
        P(dp, None),
        P(),
        P(),
        P(None, "tensor"),
        P("tensor"),
        P(None, "tensor"),
        P("tensor"),
        P(None, None, "tensor"),
        P(),
        P("tensor", None),
        P(),
        P(),
        P(),
        P(None, "tensor"),
        P(None, None, "tensor"),
        P(),
        P("tensor", None),
        P(),
        P(),
        P(),
        P(None, "tensor"),
        P("tensor"),
        P("tensor", None),
        P(),
    )
    return in_specs, out_specs


def solution(mesh):
    dp_size, size = mesh.shape["dp"], mesh.shape["tensor"]
    if dp_size == 8 and size == 4:
        grid = Mesh(mesh.devices.reshape(dp_size // 2, 2, size), ("chip", "core", "tensor"))
        in_specs, out_specs = specs(("chip", "core"))
        return jax.shard_map(
            chip_local, mesh=grid, in_specs=in_specs, out_specs=out_specs, check_vma=False
        )
    in_specs, out_specs = specs("dp")
    return jax.shard_map(
        tensor_local, mesh=mesh, in_specs=in_specs, out_specs=out_specs, check_vma=False
    )
```

```python
import functools
from functools import partial

import jax
import jax.numpy as jnp
from jax import lax
from jax.experimental import pallas as pl
from jax.experimental.pallas import tpu as pltpu
from jax.sharding import Mesh
from jax.sharding import PartitionSpec as P

HD = 88


EPSILON = 1e-06
ROPE_BASE = 10000.0
PRECISE = lax.Precision.HIGHEST


def layer_norm(values):
    center = values - jnp.mean(values, -1, keepdims=True)
    return center * lax.rsqrt(jnp.mean(center * center, -1, keepdims=True) + EPSILON)


def rope_tables(grid_pos):
    quarter = HD // 4
    frequency = ROPE_BASE ** (-jnp.arange(quarter, dtype=jnp.float32) / quarter)
    row_angle = grid_pos[..., 0:1].astype(jnp.float32) * frequency
    col_angle = grid_pos[..., 1:2].astype(jnp.float32) * frequency
    angles = jnp.concatenate([row_angle, row_angle, col_angle, col_angle], -1)
    return (jnp.cos(angles)[..., None, :], jnp.sin(angles)[..., None, :])


def rotate(values, cosines, sine_table):
    quarter = HD // 4
    first = values[..., :quarter]
    second = values[..., quarter : 2 * quarter]
    third = values[..., 2 * quarter : 3 * quarter]
    fourth = values[..., 3 * quarter :]
    turned = jnp.concatenate([-second, first, -fourth, third], -1)
    return values * cosines + turned * sine_table


def gather_tokens(values):
    return lax.all_gather(values, "tensor", axis=1, tiled=True)


def reduce_tokens(values):
    return lax.psum_scatter(
        values.astype(jnp.bfloat16), "tensor", scatter_dimension=1, tiled=True
    ).astype(jnp.float32)


def attend_forward(query_in, keys_in, values_in, key_bias):
    sequences, length, head_count, head_size = query_in.shape
    block_rows = min(512, length)
    query_blocks = jnp.moveaxis(
        query_in.reshape(sequences, length // block_rows, block_rows, head_count, head_size), 1, 0
    )

    def one_block(portion):
        scores = jnp.einsum(
            "sqhd,skhd->shqk", portion, keys_in, preferred_element_type=jnp.float32
        ) * HD ** (-0.5)
        scores = scores + key_bias[:, None, None, :]
        highest = jnp.max(scores, -1, keepdims=True)
        powers = jnp.exp(scores - highest)
        totals = jnp.sum(powers, -1, keepdims=True)
        weights = (powers / totals).astype(jnp.bfloat16)
        result = jnp.einsum(
            "shqk,skhd->sqhd", weights, values_in, preferred_element_type=jnp.float32
        )
        return (result, (highest + jnp.log(totals))[..., 0])

    results, logsum = lax.map(one_block, query_blocks)
    return (jnp.moveaxis(results, 0, 1).reshape(sequences, length, head_count * head_size), logsum)


def attend_backward(query_in, keys_in, values_in, key_bias, logsum, grad_mixed, result):
    sequences, length, head_count, head_size = query_in.shape
    block_rows = min(512, length)
    grad_heads = grad_mixed.reshape(sequences, length, head_count, head_size)
    delta = jnp.sum(
        grad_heads.astype(jnp.float32) * result.reshape(sequences, length, head_count, head_size),
        -1,
    )

    def cut_rows(array):
        return jnp.moveaxis(
            array.reshape((sequences, length // block_rows, block_rows) + array.shape[2:]), 1, 0
        )

    def one_block(running, item):
        keys_grad, values_grad = running
        portion, lse_part, grad_part, delta_part = item
        scores = jnp.einsum(
            "sqhd,skhd->shqk", portion, keys_in, preferred_element_type=jnp.float32
        ) * HD ** (-0.5)
        scores = scores + key_bias[:, None, None, :]
        weights = jnp.exp(scores - lse_part[..., None])
        values_grad = values_grad + jnp.einsum(
            "shqk,sqhd->skhd",
            weights.astype(jnp.bfloat16),
            grad_part,
            preferred_element_type=jnp.float32,
        )
        weight_grad = jnp.einsum(
            "sqhd,skhd->shqk", grad_part, values_in, preferred_element_type=jnp.float32
        )
        score_grad = (weights * (weight_grad - jnp.swapaxes(delta_part, 1, 2)[..., None])).astype(
            jnp.bfloat16
        )
        query_grad = jnp.einsum(
            "shqk,skhd->sqhd", score_grad, keys_in, preferred_element_type=jnp.float32
        ) * HD ** (-0.5)
        keys_grad = keys_grad + jnp.einsum(
            "shqk,sqhd->skhd", score_grad, portion, preferred_element_type=jnp.float32
        ) * HD ** (-0.5)
        return ((keys_grad, values_grad), query_grad)

    zero_keys = jnp.zeros(keys_in.shape, jnp.float32)
    (keys_grad, values_grad), query_grad = lax.scan(
        one_block,
        (zero_keys, zero_keys),
        (cut_rows(query_in), logsum, cut_rows(grad_heads), cut_rows(delta)),
    )
    query_grad = jnp.moveaxis(query_grad, 0, 1).reshape(query_in.shape)
    return (query_grad, keys_grad, values_grad)


def affine_norm(values, gain, beta):
    return layer_norm(values) * gain + beta


def tensor_local(
    latent_in,
    skip_in,
    text_emb,
    text_length,
    time_emb,
    grid_pos,
    skip_gain,
    skip_beta,
    skip_weight,
    skip_bias,
    ada_weight,
    ada_bias,
    query_key_value_weight,
    qk_gain,
    attention_output_weight,
    out_bias,
    norm2_gain,
    norm2_beta,
    crossed_query_weight,
    cross_kv_weight,
    cross_qk_gain,
    crossed_output_weight,
    cross_out_bias,
    norm3_gain,
    norm3_beta,
    up_projection_weight,
    up_bias,
    down_projection_weight,
    down_bias,
    out_grad,
):
    tensor_count = lax.axis_size("tensor")
    tensor_rank = lax.axis_index("tensor")
    sequences, local_len, model_width = latent_in.shape
    full_len = local_len * tensor_count
    col_width = ada_weight.shape[1]
    head_cols = query_key_value_weight.shape[2]
    local_heads = head_cols // HD
    cosines, sine_table = rope_tables(grid_pos)
    key_bias = jnp.where(
        jnp.arange(text_emb.shape[1])[None, :] < text_length[:, None], 0.0, -1e30
    ).astype(jnp.float32)
    self_bias = jnp.zeros((sequences, full_len), jnp.float32)
    skip_gain_f = skip_gain.astype(jnp.float32)
    skip_beta_f = skip_beta.astype(jnp.float32)
    norm2_gain_f = norm2_gain.astype(jnp.float32)
    norm2_beta_f = norm2_beta.astype(jnp.float32)
    norm3_gain_f = norm3_gain.astype(jnp.float32)
    norm3_beta_f = norm3_beta.astype(jnp.float32)
    qk_gain_f = qk_gain.astype(jnp.float32)
    cross_gain_f = cross_qk_gain.astype(jnp.float32)

    def first_norm(stream_in, shift_in):
        return layer_norm(stream_in) + shift_in[:, None, :]

    def qk_prep(raw, gain):
        return rotate(
            layer_norm(raw.reshape(sequences, full_len, local_heads, HD)) * gain,
            cosines,
            sine_table,
        )

    def head_norm(raw, gain):
        return layer_norm(raw.reshape(raw.shape[0], raw.shape[1], local_heads, HD)) * gain

    joined = jnp.concatenate([latent_in.astype(jnp.float32), skip_in.astype(jnp.float32)], -1)
    skip_normed = affine_norm(joined, skip_gain_f, skip_beta_f).astype(jnp.bfloat16)
    skip_all = gather_tokens(skip_normed)
    skip_cols = jnp.einsum(
        "slc,ce->sle", skip_all, skip_weight, preferred_element_type=jnp.float32
    ) + skip_bias.astype(jnp.float32)
    stream = lax.all_to_all(
        skip_cols.astype(jnp.bfloat16), "tensor", split_axis=1, concat_axis=2, tiled=True
    ).astype(skip_cols.dtype)
    condition = jax.nn.silu(time_emb.astype(jnp.float32))
    ada_weight_f = ada_weight.astype(jnp.float32)
    shift_part = jnp.dot(condition, ada_weight_f, precision=PRECISE) + ada_bias.astype(jnp.float32)
    shift_vec = lax.all_gather(shift_part, "tensor", axis=1, tiled=True)
    attn_in = first_norm(stream, shift_vec).astype(jnp.bfloat16)
    attention_gathered = gather_tokens(attn_in)
    projected = jnp.einsum(
        "mxp,jpc->jmxc",
        attention_gathered,
        query_key_value_weight,
        preferred_element_type=jnp.float32,
    )
    query_self = qk_prep(projected[0], qk_gain_f[0]).astype(jnp.bfloat16)
    keys_self = qk_prep(projected[1], qk_gain_f[1]).astype(jnp.bfloat16)
    values_self = projected[2].reshape(sequences, full_len, local_heads, HD).astype(jnp.bfloat16)
    attn_result, attn_logsum = attend_forward(query_self, keys_self, values_self, self_bias)
    attention_combined = attn_result.astype(jnp.bfloat16)
    branch_one = reduce_tokens(
        jnp.einsum(
            "jpe,ec->jpc",
            attention_combined,
            attention_output_weight,
            preferred_element_type=jnp.float32,
        )
    ) + out_bias.astype(jnp.float32)
    stream_two = stream + branch_one
    cross_in = affine_norm(stream_two, norm2_gain_f, norm2_beta_f).astype(jnp.bfloat16)
    crossed_gathered = gather_tokens(cross_in)
    query_raw = jnp.einsum(
        "pik,kx->pix", crossed_gathered, crossed_query_weight, preferred_element_type=jnp.float32
    )
    text_proj = jnp.einsum(
        "std,kdh->ksth", text_emb, cross_kv_weight, preferred_element_type=jnp.float32
    )
    cross_query = head_norm(query_raw, cross_gain_f[0]).astype(jnp.bfloat16)
    cross_keys = head_norm(text_proj[0], cross_gain_f[1]).astype(jnp.bfloat16)
    cross_values = (
        text_proj[1].reshape(sequences, text_proj.shape[2], local_heads, HD).astype(jnp.bfloat16)
    )
    cross_result, cross_logsum = attend_forward(cross_query, cross_keys, cross_values, key_bias)
    crossed_combined = cross_result.astype(jnp.bfloat16)
    branch_two = reduce_tokens(
        jnp.einsum(
            "jpe,ec->jpc",
            crossed_combined,
            crossed_output_weight,
            preferred_element_type=jnp.float32,
        )
    ) + cross_out_bias.astype(jnp.float32)
    stream_three = stream_two + branch_two
    mlp_in = affine_norm(stream_three, norm3_gain_f, norm3_beta_f).astype(jnp.bfloat16)
    gelu_fn = partial(jax.nn.gelu, approximate=True)
    perceptron_gathered = gather_tokens(mlp_in)
    hidden_pre = jnp.einsum(
        "ctk,kr->ctr", perceptron_gathered, up_projection_weight, preferred_element_type=jnp.float32
    ) + up_bias.astype(jnp.float32)
    hidden_state = gelu_fn(hidden_pre).astype(jnp.bfloat16)
    branch_three = reduce_tokens(
        jnp.einsum(
            "jgy,yv->jgv", hidden_state, down_projection_weight, preferred_element_type=jnp.float32
        )
    ) + down_bias.astype(jnp.float32)
    output = stream_three + branch_three
    stats = jnp.stack(
        [
            jnp.sqrt(jnp.mean(stream_term * stream_term, -1) + EPSILON)
            for stream_term in (stream, branch_one, branch_two, branch_three, output)
        ],
        1,
    )
    grad_out = out_grad.astype(jnp.float32)
    down_bias_part = jnp.sum(grad_out, axis=(0, 1))
    _, gelu_back = jax.vjp(gelu_fn, hidden_pre)
    gradient_gathered = gather_tokens(out_grad)
    hidden_grad = jnp.einsum(
        "bcq,eq->bce", gradient_gathered, down_projection_weight, preferred_element_type=jnp.float32
    )
    down_weight_grad = jnp.einsum(
        "mho,mhj->oj", hidden_state, gradient_gathered, preferred_element_type=jnp.float32
    )
    pre_grad = gelu_back(hidden_grad)[0]
    up_bias_grad = jnp.sum(pre_grad, axis=(0, 1))
    prenorm_reduced = pre_grad.astype(jnp.bfloat16)
    up_projection_gradient = jnp.einsum(
        "boy,bot->yt", perceptron_gathered, prenorm_reduced, preferred_element_type=jnp.float32
    )
    norm3_grad_in = reduce_tokens(
        jnp.einsum(
            "tke,ve->tkv", prenorm_reduced, up_projection_weight, preferred_element_type=jnp.float32
        )
    )
    _, norm3_back = jax.vjp(affine_norm, stream_three, norm3_gain_f, norm3_beta_f)
    from_three, gain3_part, beta3_part = norm3_back(norm3_grad_in)
    grad_three = grad_out + from_three
    cross_bias_part = jnp.sum(grad_three, axis=(0, 1))
    gradient_third_gathered = gather_tokens(grad_three.astype(jnp.bfloat16))
    cross_out_weight_grad = jnp.einsum(
        "kwy,kwn->yn", crossed_combined, gradient_third_gathered, preferred_element_type=jnp.float32
    )
    cross_mixed_grad = jnp.einsum(
        "ofz,iz->ofi",
        gradient_third_gathered,
        crossed_output_weight,
        preferred_element_type=jnp.float32,
    ).astype(jnp.bfloat16)
    cq_grad, ck_grad, cv_grad = attend_backward(
        cross_query,
        cross_keys,
        cross_values,
        key_bias,
        cross_logsum,
        cross_mixed_grad,
        cross_result,
    )
    _, cq_back = jax.vjp(head_norm, query_raw, cross_gain_f[0])
    query_raw_grad, cq_gain_part = cq_back(cq_grad)
    _, ck_back = jax.vjp(head_norm, text_proj[0], cross_gain_f[1])
    keys_raw_grad, ck_gain_part = ck_back(ck_grad)
    cross_gain_part = jnp.stack([cq_gain_part, ck_gain_part])
    query_reduced = query_raw_grad.astype(jnp.bfloat16)
    cross_query_weight_grad = jnp.einsum(
        "yfw,yfb->wb", crossed_gathered, query_reduced, preferred_element_type=jnp.float32
    )
    text_grads = jnp.stack(
        [keys_raw_grad, cv_grad.reshape(sequences, cv_grad.shape[1], head_cols)]
    ).astype(jnp.bfloat16)
    cross_kv_weight_grad = jnp.einsum(
        "std,ksth->kdh", text_emb, text_grads, preferred_element_type=jnp.float32
    )
    text_part = jnp.einsum(
        "ksth,kdh->std", text_grads, cross_kv_weight, preferred_element_type=jnp.float32
    )
    norm2_grad_in = reduce_tokens(
        jnp.einsum(
            "rjc,vc->rjv", query_reduced, crossed_query_weight, preferred_element_type=jnp.float32
        )
    )
    _, norm2_back = jax.vjp(affine_norm, stream_two, norm2_gain_f, norm2_beta_f)
    from_two, gain2_part, beta2_part = norm2_back(norm2_grad_in)
    grad_two = grad_three + from_two
    out_bias_part = jnp.sum(grad_two, axis=(0, 1))
    gradient_second_gathered = gather_tokens(grad_two.astype(jnp.bfloat16))
    out_weight_grad = jnp.einsum(
        "kwy,kwn->yn",
        attention_combined,
        gradient_second_gathered,
        preferred_element_type=jnp.float32,
    )
    attn_mixed_grad = jnp.einsum(
        "ofz,iz->ofi",
        gradient_second_gathered,
        attention_output_weight,
        preferred_element_type=jnp.float32,
    ).astype(jnp.bfloat16)
    sq_grad, sk_grad, sv_grad = attend_backward(
        query_self, keys_self, values_self, self_bias, attn_logsum, attn_mixed_grad, attn_result
    )
    _, sq_back = jax.vjp(qk_prep, projected[0], qk_gain_f[0])
    q_raw_grad, sq_gain_part = sq_back(sq_grad)
    _, sk_back = jax.vjp(qk_prep, projected[1], qk_gain_f[1])
    k_raw_grad, sk_gain_part = sk_back(sk_grad)
    self_gain_part = jnp.stack([sq_gain_part, sk_gain_part])
    projection_gradient = jnp.stack(
        [q_raw_grad, k_raw_grad, sv_grad.reshape(sequences, full_len, head_cols)]
    ).astype(jnp.bfloat16)
    qkv_weight_grad = jnp.einsum(
        "yze,myzi->mei", attention_gathered, projection_gradient, preferred_element_type=jnp.float32
    )
    first_grad_in = reduce_tokens(
        jnp.einsum(
            "apwf,acf->pwc",
            projection_gradient,
            query_key_value_weight,
            preferred_element_type=jnp.float32,
        )
    )
    _, first_back = jax.vjp(first_norm, stream, shift_vec)
    from_one, shift_part_grad = first_back(first_grad_in)
    grad_one = grad_two + from_one
    (
        shift_grad,
        down_bias_sum,
        gain3_sum,
        beta3_sum,
        cross_bias_sum,
        gain2_sum,
        beta2_sum,
        cross_gain_sum,
        out_bias_sum,
        self_gain_sum,
    ) = (
        lax.psum(shift_part_grad.astype(jnp.bfloat16), "tensor").astype(jnp.float32),
        lax.psum(down_bias_part.astype(jnp.bfloat16), "tensor").astype(jnp.float32),
        lax.psum(gain3_part.astype(jnp.bfloat16), "tensor").astype(jnp.float32),
        lax.psum(beta3_part.astype(jnp.bfloat16), "tensor").astype(jnp.float32),
        lax.psum(cross_bias_part.astype(jnp.bfloat16), "tensor").astype(jnp.float32),
        lax.psum(gain2_part.astype(jnp.bfloat16), "tensor").astype(jnp.float32),
        lax.psum(beta2_part.astype(jnp.bfloat16), "tensor").astype(jnp.float32),
        lax.psum(cross_gain_part.astype(jnp.bfloat16), "tensor").astype(jnp.float32),
        lax.psum(out_bias_part.astype(jnp.bfloat16), "tensor").astype(jnp.float32),
        lax.psum(self_gain_part.astype(jnp.bfloat16), "tensor").astype(jnp.float32),
    )
    shift_cols = lax.dynamic_slice_in_dim(shift_grad, tensor_rank * col_width, col_width, 1)
    ada_bias_grad = jnp.sum(shift_cols, axis=0)
    ada_weight_grad = jnp.dot(condition.T, shift_cols, precision=PRECISE)
    condition_grad = jnp.dot(shift_cols, ada_weight_f.T, precision=PRECISE)
    _, silu_back = jax.vjp(jax.nn.silu, time_emb.astype(jnp.float32))
    time_part = silu_back(condition_grad)[0]
    skip_grad_cols = lax.all_to_all(
        grad_one.astype(jnp.bfloat16), "tensor", split_axis=2, concat_axis=1, tiled=True
    ).astype(grad_one.dtype)
    skip_bias_grad = jnp.sum(skip_grad_cols, axis=(0, 1))
    skip_low = skip_grad_cols.astype(jnp.bfloat16)
    skip_weight_grad = jnp.einsum(
        "slc,sle->ce", skip_all, skip_low, preferred_element_type=jnp.float32
    )
    joined_grad_in = reduce_tokens(
        jnp.einsum("sle,ce->slc", skip_low, skip_weight, preferred_element_type=jnp.float32)
    )
    _, skip_norm_back = jax.vjp(affine_norm, joined, skip_gain_f, skip_beta_f)
    joined_grad, skip_gain_part, skip_beta_part = skip_norm_back(joined_grad_in)
    latent_grad = joined_grad[..., :model_width]
    skip_grad = joined_grad[..., model_width:]
    text_grad, time_grad, skip_gain_sum, skip_beta_sum = (
        lax.psum(text_part.astype(jnp.bfloat16), "tensor").astype(jnp.float32),
        lax.psum(time_part.astype(jnp.bfloat16), "tensor").astype(jnp.float32),
        lax.psum(skip_gain_part.astype(jnp.bfloat16), "tensor").astype(jnp.float32),
        lax.psum(skip_beta_part.astype(jnp.bfloat16), "tensor").astype(jnp.float32),
    )
    weight_sums = (
        lax.psum(skip_gain_sum.astype(jnp.bfloat16), "dp").astype(jnp.float32),
        lax.psum(skip_beta_sum.astype(jnp.bfloat16), "dp").astype(jnp.float32),
        lax.psum(skip_weight_grad.astype(jnp.bfloat16), "dp").astype(jnp.float32),
        lax.psum(skip_bias_grad.astype(jnp.bfloat16), "dp").astype(jnp.float32),
        lax.psum(ada_weight_grad.astype(jnp.bfloat16), "dp").astype(jnp.float32),
        lax.psum(ada_bias_grad.astype(jnp.bfloat16), "dp").astype(jnp.float32),
        lax.psum(qkv_weight_grad.astype(jnp.bfloat16), "dp").astype(jnp.float32),
        lax.psum(self_gain_sum.astype(jnp.bfloat16), "dp").astype(jnp.float32),
        lax.psum(out_weight_grad.astype(jnp.bfloat16), "dp").astype(jnp.float32),
        lax.psum(out_bias_sum.astype(jnp.bfloat16), "dp").astype(jnp.float32),
        lax.psum(gain2_sum.astype(jnp.bfloat16), "dp").astype(jnp.float32),
        lax.psum(beta2_sum.astype(jnp.bfloat16), "dp").astype(jnp.float32),
        lax.psum(cross_query_weight_grad.astype(jnp.bfloat16), "dp").astype(jnp.float32),
        lax.psum(cross_kv_weight_grad.astype(jnp.bfloat16), "dp").astype(jnp.float32),
        lax.psum(cross_gain_sum.astype(jnp.bfloat16), "dp").astype(jnp.float32),
        lax.psum(cross_out_weight_grad.astype(jnp.bfloat16), "dp").astype(jnp.float32),
        lax.psum(cross_bias_sum.astype(jnp.bfloat16), "dp").astype(jnp.float32),
        lax.psum(gain3_sum.astype(jnp.bfloat16), "dp").astype(jnp.float32),
        lax.psum(beta3_sum.astype(jnp.bfloat16), "dp").astype(jnp.float32),
        lax.psum(up_projection_gradient.astype(jnp.bfloat16), "dp").astype(jnp.float32),
        lax.psum(up_bias_grad.astype(jnp.bfloat16), "dp").astype(jnp.float32),
        lax.psum(down_weight_grad.astype(jnp.bfloat16), "dp").astype(jnp.float32),
        lax.psum(down_bias_sum.astype(jnp.bfloat16), "dp").astype(jnp.float32),
    )
    return (
        output.astype(jnp.bfloat16),
        stats,
        latent_grad,
        skip_grad,
        text_grad,
        time_grad,
    ) + tuple(weight_sums)


LANES = 128
LOG2E = 1.4426950408889634


def lane_index(shape):
    return lax.broadcasted_iota(jnp.int32, shape, 1)


def matmul_nt(left, right):
    return lax.dot_general(left, right, (((1,), (1,)), ((), ())), preferred_element_type=jnp.float32)


def matmul_nn(left, right):
    return lax.dot_general(left, right, (((1,), (0,)), ((), ())), preferred_element_type=jnp.float32)


def matmul_tn(left, right):
    return lax.dot_general(left, right, (((0,), (0,)), ((), ())), preferred_element_type=jnp.float32)


def row_sums(rows, both_parts=False):
    ones = jnp.ones((LANES, LANES), jnp.bfloat16)
    high = rows.astype(jnp.bfloat16)
    total = matmul_nn(high, ones)
    if both_parts:
        total = total + matmul_nn((rows - high.astype(jnp.float32)).astype(jnp.bfloat16), ones)
    return total


def norm_rows(raw):
    center = raw - row_sums(raw, True) * (1.0 / HD)
    center = jnp.where(lane_index(raw.shape) < HD, center, 0.0)
    inverse = lax.rsqrt(row_sums(center * center) * (1.0 / HD) + EPSILON)
    return center * inverse, inverse


def norm_rows_back(grad, normed, inverse):
    mean = row_sums(grad) * (1.0 / HD)
    along = row_sums(grad * normed) * (1.0 / HD)
    return jnp.where(lane_index(grad.shape) < HD, inverse * (grad - mean - normed * along), 0.0)


def turn_rows(rows, tables):
    quarter = HD // 4
    return (
        rows * tables[0]
        + pltpu.roll(rows, LANES - quarter, 1) * tables[1]
        + pltpu.roll(rows, quarter, 1) * tables[2]
    )


def turn_rows_back(grad, tables):
    quarter = HD // 4
    return (
        grad * tables[0]
        + pltpu.roll(grad * tables[1], quarter, 1)
        + pltpu.roll(grad * tables[2], LANES - quarter, 1)
    )


def kept_keys(count_ref, shape):
    return lax.broadcasted_iota(jnp.int32, shape, 0).astype(jnp.float32) < count_ref[0:1, :]


def attention_kernel(turned, rows, *refs):
    if turned:
        q_ref, k_ref, v_ref, gain_ref, count_ref, table_ref, out_ref, exact_ref, inv_ref = refs
    else:
        q_ref, k_ref, v_ref, gain_ref, count_ref, out_ref, exact_ref, inv_ref = refs
    low = jnp.bfloat16
    keys = norm_rows(k_ref[...])[0] * gain_ref[1:2, :]
    if turned:
        keys = turn_rows(keys, (table_ref[0], table_ref[1], table_ref[2]))
    values = v_ref[...]
    ones = jnp.ones(values.shape, jnp.float32)
    if not turned:
        kept = kept_keys(count_ref, values.shape)
        keys = jnp.where(kept, keys, 0.0)
        values = jnp.where(kept, values, 0.0)
        ones = jnp.where(kept, ones, 0.0)
    keys = keys.astype(low)
    mixed = jnp.concatenate([values.astype(low), ones.astype(low)], 1)
    for start in range(0, q_ref.shape[0], rows):
        part = pl.ds(start, rows)
        query = norm_rows(q_ref[part, :])[0] * gain_ref[0:1, :]
        if turned:
            query = turn_rows(query, tuple(table_ref[i, part, :] for i in range(3)))
        powers = jnp.exp2(matmul_nt(query.astype(low), keys)).astype(low)
        sums = matmul_nn(powers, mixed)
        inverse = 1.0 / sums[:, LANES:]
        result = sums[:, :LANES] * inverse
        out_ref[part, :] = result.astype(low)
        exact_ref[part, :] = result
        inv_ref[part, :] = inverse


def attention_back_kernel(turned, rows, *refs):
    if turned:
        q_ref, k_ref, v_ref, gain_ref, count_ref, table_ref = refs[:6]
        refs = refs[6:]
    else:
        q_ref, k_ref, v_ref, gain_ref, count_ref = refs[:5]
        refs = refs[5:]
    grad_ref, out_ref, inv_ref, dq_ref, dk_ref, dv_ref, dgain_ref, keys_acc, values_acc = refs
    low = jnp.bfloat16
    f32 = jnp.float32
    key_normed, key_inverse = norm_rows(k_ref[...])
    keys = key_normed * gain_ref[1:2, :]
    if turned:
        keys = turn_rows(keys, (table_ref[0], table_ref[1], table_ref[2]))
    else:
        kept = kept_keys(count_ref, keys.shape)
        keys = jnp.where(kept, keys, 0.0)
    keys = keys.astype(low)
    lane = lane_index(k_ref.shape)
    values = jnp.where((lane == HD) | (lane == HD + 1), 1.0, v_ref[...]).astype(low)
    factor = HD ** (-0.5)
    gain_total = jnp.zeros((1, LANES), f32)
    for start in range(0, q_ref.shape[0], rows):
        part = pl.ds(start, rows)
        query_normed, query_inverse = norm_rows(q_ref[part, :])
        query = query_normed * gain_ref[0:1, :]
        if turned:
            tables = tuple(table_ref[i, part, :] for i in range(3))
            query = turn_rows(query, tables)
        query = query.astype(low)
        grad = grad_ref[part, :].astype(f32) * inv_ref[part, :]
        grad_low = grad.astype(low)
        delta = row_sums(grad_low.astype(f32) * out_ref[part, :], True)
        delta_high = delta.astype(low).astype(f32)
        lane = lane_index((rows, LANES))
        grad_more = jnp.where(
            lane == HD, -delta_high, jnp.where(lane == HD + 1, delta_high - delta, grad)
        ).astype(low)
        powers = jnp.exp2(matmul_nt(keys, query))
        score_grad = (powers * matmul_nt(values, grad_more)).astype(low)
        values_part = matmul_nn(powers.astype(low), grad_low)
        keys_part = matmul_nn(score_grad, query)
        if start == 0:
            values_acc[...] = values_part
            keys_acc[...] = keys_part
        else:
            values_acc[...] += values_part
            keys_acc[...] += keys_part
        query_grad = matmul_tn(score_grad, keys) * factor
        if turned:
            query_grad = turn_rows_back(query_grad, tables)
        gain_total = gain_total + jnp.sum(query_grad * query_normed, 0, keepdims=True)
        dq_ref[part, :] = norm_rows_back(
            query_grad * gain_ref[2:3, :], query_normed, query_inverse
        ).astype(low)
    values_grad = values_acc[...]
    key_grad = keys_acc[...] * (1.0 / LOG2E)
    if turned:
        key_grad = turn_rows_back(key_grad, (table_ref[0], table_ref[1], table_ref[2]))
    else:
        kept = kept_keys(count_ref, key_grad.shape)
        values_grad = jnp.where(kept, values_grad, 0.0)
        key_grad = jnp.where(kept, key_grad, 0.0)
    dv_ref[...] = values_grad.astype(low)
    dk_ref[...] = norm_rows_back(key_grad * gain_ref[1:2, :], key_normed, key_inverse).astype(low)
    dgain_ref[0, 0:1, :] = gain_total
    dgain_ref[0, 1:2, :] = jnp.sum(key_grad * key_normed, 0, keepdims=True)
    dgain_ref[0, 2:8, :] = jnp.zeros((6, LANES), f32)


def attention_specs(turned, length, key_length, q_at, k_at, v_at):
    specs = [
        pl.BlockSpec((length, LANES), lambda h: (0, q_at + h)),
        pl.BlockSpec((key_length, LANES), lambda h: (0, k_at + h)),
        pl.BlockSpec((key_length, LANES), lambda h: (0, v_at + h)),
        pl.BlockSpec((8, LANES), lambda h: (0, 0)),
        pl.BlockSpec((8, LANES), lambda h: (0, 0)),
    ]
    if turned:
        specs.append(pl.BlockSpec((3, length, LANES), lambda h: (0, 0, 0)))
    return specs


def attention(heads, query, keys, values, at, gains, count, tables=None, rows=256):
    length, key_length = query.shape[0], keys.shape[0]
    turned = tables is not None
    operands = [query, keys, values, gains, count] + ([tables] if turned else [])
    pairs = heads * length * key_length
    return pl.pallas_call(
        functools.partial(attention_kernel, turned, min(rows, length)),
        grid=(heads,),
        in_specs=attention_specs(turned, length, key_length, *at),
        out_specs=[pl.BlockSpec((length, LANES), lambda h: (0, h))] * 3,
        out_shape=[
            jax.ShapeDtypeStruct((length, heads * LANES), jnp.bfloat16),
            jax.ShapeDtypeStruct((length, heads * LANES), jnp.float32),
            jax.ShapeDtypeStruct((length, heads * LANES), jnp.float32),
        ],
        compiler_params=pltpu.CompilerParams(
            dimension_semantics=("arbitrary",), vmem_limit_bytes=40 * 2**20
        ),
        cost_estimate=pl.CostEstimate(
            flops=4 * pairs * LANES, transcendentals=pairs, bytes_accessed=22 * heads * length * LANES
        ),
        name="attention_turned" if turned else "attention_plain",
    )(*operands)


def attention_back(
    heads, query, keys, values, at, gains, count, grad, mixed, inverse, tables=None, rows=256
):
    length, key_length = query.shape[0], keys.shape[0]
    turned = tables is not None
    operands = [query, keys, values, gains, count] + ([tables] if turned else [])
    pairs = heads * length * key_length
    return pl.pallas_call(
        functools.partial(attention_back_kernel, turned, min(rows, length)),
        grid=(heads,),
        in_specs=attention_specs(turned, length, key_length, *at)
        + [pl.BlockSpec((length, LANES), lambda h: (0, h))] * 3,
        out_specs=[
            pl.BlockSpec((length, LANES), lambda h: (0, h)),
            pl.BlockSpec((key_length, LANES), lambda h: (0, h)),
            pl.BlockSpec((key_length, LANES), lambda h: (0, h)),
            pl.BlockSpec((1, 8, LANES), lambda h: (h, 0, 0)),
        ],
        out_shape=[
            jax.ShapeDtypeStruct((length, heads * LANES), jnp.bfloat16),
            jax.ShapeDtypeStruct((key_length, heads * LANES), jnp.bfloat16),
            jax.ShapeDtypeStruct((key_length, heads * LANES), jnp.bfloat16),
            jax.ShapeDtypeStruct((heads, 8, LANES), jnp.float32),
        ],
        scratch_shapes=[
            pltpu.VMEM((key_length, LANES), jnp.float32),
            pltpu.VMEM((key_length, LANES), jnp.float32),
        ],
        compiler_params=pltpu.CompilerParams(
            dimension_semantics=("arbitrary",), vmem_limit_bytes=40 * 2**20
        ),
        cost_estimate=pl.CostEstimate(
            flops=10 * pairs * LANES, transcendentals=pairs, bytes_accessed=32 * heads * length * LANES
        ),
        name="attention_turned_back" if turned else "attention_plain_back",
    )(*operands, grad, mixed, inverse)


def ring_pairs(size, step):
    return [(rank, (rank + step) % size) for rank in range(size)]


def swap_cores(values):
    return lax.ppermute(values, "core", [(0, 1), (1, 0)])


def from_later(values, step, size):
    return lax.ppermute(values, "tensor", ring_pairs(size, -step))


def from_earlier(values, step, size):
    return lax.ppermute(values, "tensor", ring_pairs(size, step))


def spread_pairs(size, turn):
    pairs = []
    for core in range(2):
        for rank in range(size):
            piece = (rank + turn) % size
            pairs.append((core * size + rank, (piece % 2) * size + 2 * core + piece // 2))
    return pairs


def pick(array, index):
    return lax.dynamic_index_in_dim(array, index, 0, keepdims=False)


def rolled(array, start):
    return lax.dynamic_slice_in_dim(jnp.concatenate([array, array], 0), start, array.shape[0], 0)


def tie(*values):
    return lax.optimization_barrier(values)


def dot_tt(left, right):
    return lax.dot_general(left, right, (((1,), (1,)), ((), ())), preferred_element_type=jnp.float32)


def dot_nn(left, right):
    return lax.dot_general(left, right, (((1,), (0,)), ((), ())), preferred_element_type=jnp.float32)


def dot_tn(left, right):
    return lax.dot_general(left, right, (((0,), (0,)), ((), ())), preferred_element_type=jnp.float32)


def chip_local(
    latent_in,
    skip_in,
    text_emb,
    text_length,
    time_emb,
    grid_pos,
    skip_gain,
    skip_beta,
    skip_weight,
    skip_bias,
    ada_weight,
    ada_bias,
    query_key_value_weight,
    qk_gain,
    attention_output_weight,
    out_bias,
    norm2_gain,
    norm2_beta,
    crossed_query_weight,
    cross_kv_weight,
    cross_qk_gain,
    crossed_output_weight,
    cross_out_bias,
    norm3_gain,
    norm3_beta,
    up_projection_weight,
    up_bias,
    down_projection_weight,
    down_bias,
    out_grad,
):
    f32 = jnp.float32
    low = jnp.bfloat16
    size = lax.axis_size("tensor")
    chips = lax.axis_size("chip")
    rank = lax.axis_index("tensor")
    core = lax.axis_index("core")
    chip = lax.axis_index("chip")
    sequences, local_len, width = latent_in.shape
    piece_len = local_len // 2
    own_len = size * piece_len
    shard = ada_weight.shape[1]
    half = shard // 2
    heads = size * half // HD
    ff_half = up_bias.shape[0] // 2
    ff_part = ff_half // chips
    lanes = heads * LANES
    at_home = core == rank // sequences

    def spread(values):
        return jnp.stack(
            [
                lax.ppermute(
                    pick(values, (rank + turn) % size), ("core", "tensor"), spread_pairs(size, turn)
                )
                for turn in range(size)
            ]
        )

    def collect(values):
        parts = [
            lax.ppermute(
                values[turn],
                ("core", "tensor"),
                [(target, source) for source, target in spread_pairs(size, turn)],
            )
            for turn in range(size)
        ]
        return rolled(jnp.stack(parts), (size - rank) % size)

    def of_sequence(values):
        mine = pick(values, rank % sequences)
        return jnp.where(at_home, mine, swap_cores(mine))

    def both(values):
        return jnp.concatenate([values, swap_cores(values)], 0)

    def halve(values):
        return values[:own_len] + swap_cores(values[own_len:].astype(low)).astype(f32)

    def quarters(owns):
        mine = jnp.concatenate([pick(own, chip) for own in owns], 0)
        later = jnp.stack([from_later(mine, step, size) for step in range(1, size)])
        parts, at = [], 0
        for own in owns:
            parts.append(later[:, at : at + own.shape[1]])
            at += own.shape[1]
        return parts

    def gather_shares(later):
        return lax.all_gather(later, "chip", axis=0, tiled=False)

    def gather_all(part):
        return lax.all_gather(part, ("chip", "tensor"), axis=0, tiled=True)

    def pad_heads(own, rest):
        own = own.reshape(own.shape[0], 1, half // HD, HD, width)
        rest = rest.reshape(own.shape[0], size - 1, half // HD, HD, width)
        zero = jnp.zeros((), low)
        nothing = (0, 0, 0)
        own = lax.pad(own, zero, (nothing, (0, size - 1, 0), nothing, (0, LANES - HD, 0), nothing))
        rest = lax.pad(rest, zero, (nothing, (1, 0, 0), nothing, (0, LANES - HD, 0), nothing))
        return (own + rest).reshape(-1, lanes, width)

    def trim_heads(rows):
        return rows.reshape(heads, LANES, width)[:, :HD].reshape(size, half, width)

    def by_core(own):
        other = swap_cores(own)
        return jnp.where(core == 0, own, other), jnp.where(core == 0, other, own)

    def scatter_rows(partial_sums):
        rows = partial_sums.shape[2]
        return lax.psum_scatter(
            partial_sums.reshape(chips * size * rows, width), "chip", scatter_dimension=0, tiled=True
        ).reshape(size, rows, width)

    def send_line(parts):
        return [from_earlier(parts[step], step, size) for step in range(1, size)]

    def add_line(own, arrived):
        total = own.astype(f32)
        for part in arrived:
            total = total + part.astype(f32)
        return total.astype(low)

    def share_rows(total):
        return lax.all_gather(total, "chip", axis=0, tiled=True)

    def half_cols(weight):
        return lax.dynamic_slice_in_dim(weight, core * half, half, 1).T

    def half_rows(weight):
        return lax.dynamic_slice_in_dim(weight, core * half, half, 0)

    skip_half = lax.dynamic_slice_in_dim(skip_weight, core * width, width, 0).T
    skip_part = shard // chips
    (skip_later,) = quarters([skip_half.reshape(chips, skip_part, width)])
    skip_mine = pick(skip_half.reshape(chips, skip_part, width), chip)
    skip_abs = rolled(jnp.concatenate([skip_mine[None], skip_later], 0), (size - rank) % size)
    skip_own_w = gather_shares(skip_abs).transpose(1, 0, 2, 3).reshape(width, width)

    self_own = jnp.stack(
        [half_cols(query_key_value_weight[i]) for i in range(3)]
        + [half_rows(attention_output_weight)]
    )
    cross_own = jnp.stack(
        [half_cols(crossed_query_weight), half_cols(cross_kv_weight[0]), half_cols(cross_kv_weight[1])]
        + [half_rows(crossed_output_weight)]
    )
    up_own = lax.dynamic_slice_in_dim(up_projection_weight, core * ff_half, ff_half, 1).T
    up_own = up_own.reshape(chips, ff_part, width)
    down_own = lax.dynamic_slice_in_dim(down_projection_weight, core * ff_half, ff_half, 0)
    down_own = down_own.reshape(chips, ff_part, width)
    skip_other_w = swap_cores(skip_own_w)
    condition = jax.nn.silu(time_emb.astype(f32))
    ada_weight_f = ada_weight.astype(f32)
    shift_part = jnp.dot(condition, ada_weight_f, precision=PRECISE) + ada_bias.astype(f32)
    shift_part = shift_part.reshape(sequences * shard)
    shift_high = shift_part.astype(low)
    shift_low = (shift_part - shift_high.astype(f32)).astype(low)
    up_bias_own = lax.dynamic_slice_in_dim(up_bias, core * ff_half, ff_half, 0)
    small = jnp.concatenate([shift_high, shift_low, skip_bias, up_bias_own])
    small_size = small.shape[0]
    small_rows = 8 * -(-small_size // (8 * width))
    small = jnp.pad(small, (0, small_rows * width - small_size)).reshape(1, small_rows, width)
    small = jnp.broadcast_to(small, (chips, small_rows, width))
    self_later, small_later = quarters([self_own, small])
    self_later, cross_own = tie(self_later, cross_own)
    (cross_later,) = quarters([cross_own])
    cross_later, grad_home = tie(cross_later, out_grad)
    self_rest = gather_shares(self_later)
    self_in_w = pad_heads(self_own[:3], self_rest[:3]).reshape(3 * lanes, width)
    self_out_w = pad_heads(self_own[3:], self_rest[3:])[0]
    cross_rest = gather_shares(cross_later)
    cross_query_w = pad_heads(cross_own[:1], cross_rest[:1])[0]
    cross_text_w = pad_heads(cross_own[1:3], cross_rest[1:3]).reshape(2 * lanes, width)
    cross_out_w = pad_heads(cross_own[3:], cross_rest[3:])[0]
    up_full = gather_all(pick(up_own, chip))
    down_full = gather_all(pick(down_own, chip))

    small_rel = jnp.concatenate([small[:1], small_later], 0).reshape(size, -1)[:, :small_size].astype(f32)
    shift_size = sequences * shard
    up_bias_f = (
        rolled(small_rel[:, 2 * shift_size + shard :], (size - rank) % size)
        .reshape(size, chips, ff_part)
        .transpose(1, 0, 2)
        .reshape(size * ff_half)
    )
    small_rel = jnp.concatenate(
        [
            small_rel[:, :shift_size] + small_rel[:, shift_size : 2 * shift_size],
            small_rel[:, 2 * shift_size : 2 * shift_size + shard],
        ],
        1,
    )
    small_abs = rolled(small_rel, (size - rank) % size)
    small_abs = small_abs.reshape(size, sequences + 1, shard).transpose(1, 0, 2)
    small_abs = small_abs.reshape(sequences + 1, width)
    skip_bias_f = small_abs[sequences]
    full_len = grid_pos.shape[1]
    of_mine = of_sequence(
        jnp.concatenate(
            [
                small_abs[:sequences],
                text_length.astype(f32)[:, None],
                grid_pos.astype(f32).transpose(0, 2, 1).reshape(sequences, 2 * full_len),
            ],
            1,
        )
    )
    shift_vec = of_mine[:width]
    key_count = jnp.broadcast_to(of_mine[width], (8, LANES))
    positions = of_mine[width + 1 :].reshape(2, 2 * size, piece_len)
    text_own = of_sequence(text_emb)
    text_size = text_own.shape[0]

    by_piece = positions.transpose(1, 0, 2)

    def piece_index(of_core, turn):
        source = (2 * (rank % 2) + of_core - turn) % size
        return source * 2 + of_core

    ordered = jnp.concatenate(
        [pick(by_piece, piece_index(of_core, turn)) for of_core in (core, 1 - core) for turn in range(size)],
        1,
    )
    lane = jnp.arange(LANES)
    quarter = lane // (HD // 4)
    frequency = ROPE_BASE ** (-(lane % (HD // 4)).astype(f32) / (HD // 4))
    angles = ordered[0][:, None] * jnp.where(quarter < 2, frequency, 0.0)[None, :]
    angles = angles + ordered[1][:, None] * jnp.where(quarter < 2, 0.0, frequency)[None, :]
    real_lane = lane < HD
    sines = jnp.sin(angles)
    tables = jnp.stack(
        [
            jnp.where(real_lane, jnp.cos(angles), 0.0),
            jnp.where(real_lane & (quarter % 2 == 0), -sines, 0.0),
            jnp.where(real_lane & (quarter % 2 == 1), sines, 0.0),
        ]
    )

    def kernel_gains(gains):
        rows = jnp.stack([gains[0] * (HD ** (-0.5) * LOG2E), gains[1], gains[0]])
        return jnp.pad(rows, ((0, 5), (0, LANES - HD)))

    skip_gain_f = skip_gain.astype(f32)
    skip_beta_f = skip_beta.astype(f32)
    norm2_gain_f = norm2_gain.astype(f32)
    norm2_beta_f = norm2_beta.astype(f32)
    norm3_gain_f = norm3_gain.astype(f32)
    norm3_beta_f = norm3_beta.astype(f32)

    def first_norm(stream_in, shift_in):
        return layer_norm(stream_in) + shift_in[None, :]

    self_gains = kernel_gains(qk_gain.astype(f32))
    cross_gains = kernel_gains(cross_qk_gain.astype(f32))

    latent_f = latent_in.reshape(own_len, width).astype(f32)
    skip_f = skip_in.reshape(own_len, width).astype(f32)
    joined_size = 2 * width
    center = (jnp.sum(latent_f, -1, keepdims=True) + jnp.sum(skip_f, -1, keepdims=True)) / joined_size
    latent_c = latent_f - center
    skip_c = skip_f - center
    spread_sq = jnp.sum(latent_c * latent_c, -1, keepdims=True) + jnp.sum(
        skip_c * skip_c, -1, keepdims=True
    )
    inverse = lax.rsqrt(spread_sq / joined_size + EPSILON)
    normed = jnp.stack(
        [
            (latent_c * inverse * skip_gain_f[:width] + skip_beta_f[:width]).astype(low),
            (skip_c * inverse * skip_gain_f[width:] + skip_beta_f[width:]).astype(low),
        ]
    )
    normed_own = pick(normed, core)
    normed_other = pick(normed, 1 - core)
    stream_home = (
        dot_tt(normed_own, skip_own_w) + dot_tt(normed_other, skip_other_w) + skip_bias_f
    ).astype(low)
    stream_low = spread(stream_home.reshape(size, piece_len, width)).reshape(own_len, width)
    stream = stream_low.astype(f32)

    grad_low = spread(grad_home.reshape(size, piece_len, width)).reshape(own_len, width)
    attn_own, grad_low = tie(first_norm(stream, shift_vec).astype(low), grad_low)
    attn_in = both(attn_own)
    projected = dot_tt(attn_in, self_in_w)
    self_inputs = (heads, projected, projected, projected, (0, heads, 2 * heads), self_gains, key_count)
    attention_combined, self_exact, self_inverse = attention(*self_inputs, tables, rows=2 * own_len)
    branch_one = halve(dot_nn(attention_combined, self_out_w)) + out_bias.astype(f32)
    stream_two = stream + branch_one
    cross_in = both(affine_norm(stream_two, norm2_gain_f, norm2_beta_f).astype(low))
    query_raw = dot_tt(cross_in, cross_query_w)
    text_raw = dot_tt(text_own, cross_text_w)
    cross_inputs = (heads, query_raw, text_raw, text_raw, (0, 0, heads), cross_gains, key_count)
    crossed_combined, cross_exact, cross_inverse = attention(*cross_inputs, rows=2 * own_len)
    branch_two = halve(dot_nn(crossed_combined, cross_out_w)) + cross_out_bias.astype(f32)
    stream_three = stream_two + branch_two
    mlp_in = both(affine_norm(stream_three, norm3_gain_f, norm3_beta_f).astype(low))
    gelu_fn = partial(jax.nn.gelu, approximate=True)
    hidden_pre = dot_tt(mlp_in, up_full) + up_bias_f
    hidden_state, gelu_back = jax.vjp(gelu_fn, hidden_pre)
    hidden_state = hidden_state.astype(low)
    branch_three = halve(dot_nn(hidden_state, down_full)) + down_bias.astype(f32)
    output = stream_three + branch_three
    stats = jnp.stack(
        [
            jnp.sqrt(jnp.mean(term * term, -1) + EPSILON)
            for term in (stream, branch_one, branch_two, branch_three, output)
        ]
    )
    stat_rows = stats.reshape(5, size, piece_len).transpose(1, 0, 2).reshape(size, 1, 5 * piece_len)
    stat_rows = jnp.pad(stat_rows.astype(low), ((0, 0), (0, 7), (0, width - 5 * piece_len)))
    home_rows = jnp.concatenate([output.astype(low).reshape(size, piece_len, width), stat_rows], 1)

    grad_out = grad_low.astype(f32)
    down_bias_part = jnp.sum(grad_out, axis=0)
    grad_all = both(grad_low)
    down_grad = dot_tn(hidden_state, grad_all).astype(low)
    grad_all, down_grad = tie(grad_all, down_grad)
    down_parts = rolled(scatter_rows(down_grad.reshape(chips, size, ff_part, width)), rank)
    hidden_grad = dot_tt(grad_all, down_full)
    pre_grad = gelu_back(hidden_grad)[0]
    up_bias_part = jnp.sum(pre_grad, axis=0)
    pre_low = pre_grad.astype(low)
    up_grad = dot_tn(pre_low, mlp_in).astype(low)
    pre_low, up_grad = tie(pre_low, up_grad)
    norm3_grad_in = halve(dot_nn(pre_low, up_full))
    _, norm3_back = jax.vjp(affine_norm, stream_three, norm3_gain_f, norm3_beta_f)
    from_three, gain3_part, beta3_part = norm3_back(norm3_grad_in)
    grad_three = grad_out + from_three
    cross_bias_part = jnp.sum(grad_three, axis=0)
    three_all = both(grad_three.astype(low))
    cross_out_grad = dot_tn(crossed_combined, three_all)
    cross_mixed_grad = dot_tt(three_all, cross_out_w).astype(low)
    up_grad, down_parts, cross_mixed_grad = tie(up_grad, down_parts, cross_mixed_grad)
    up_parts = rolled(scatter_rows(up_grad.reshape(chips, size, ff_part, width)), rank)
    query_low, keys_low, values_low, cross_gain_sums = attention_back(
        *cross_inputs, cross_mixed_grad, cross_exact, cross_inverse, rows=2 * own_len
    )
    down_total = add_line(down_parts[0], send_line(down_parts))
    query_low, keys_low, values_low, down_total = tie(query_low, keys_low, values_low, down_total)
    norm2_grad_in = halve(dot_nn(query_low, cross_query_w))
    cross_grads = jnp.stack(
        [
            trim_heads(grad.astype(low))
            for grad in (
                dot_tn(query_low, cross_in),
                dot_tn(keys_low, text_own),
                dot_tn(values_low, text_own),
                cross_out_grad,
            )
        ],
    )
    text_part = dot_nn(keys_low, cross_text_w[:lanes]) + dot_nn(values_low, cross_text_w[lanes:])
    _, norm2_back = jax.vjp(affine_norm, stream_two, norm2_gain_f, norm2_beta_f)
    from_two, gain2_part, beta2_part = norm2_back(norm2_grad_in)
    grad_two = grad_three + from_two
    out_bias_part = jnp.sum(grad_two, axis=0)
    two_all = both(grad_two.astype(low))
    out_weight_part = dot_tn(attention_combined, two_all)
    attn_mixed_grad = dot_tt(two_all, self_out_w).astype(low)
    home = collect(home_rows)
    cross_grads, up_parts, attn_mixed_grad, home = tie(cross_grads, up_parts, attn_mixed_grad, home)
    output_home = home[:, :piece_len].reshape(latent_in.shape)
    stats_home = (
        home[:, piece_len, : 5 * piece_len]
        .reshape(sequences, 2, 5, piece_len)
        .transpose(0, 2, 1, 3)
        .reshape(sequences, 5, local_len)
        .astype(f32)
    )
    cross_parts = scatter_rows(cross_grads)
    *proj_grads, self_gain_sums = attention_back(
        *self_inputs, attn_mixed_grad, self_exact, self_inverse, tables, rows=2 * own_len
    )
    up_total = add_line(up_parts[0], send_line(up_parts))
    *proj_grads, up_total = tie(*proj_grads, up_total)
    first_grad_in = halve(
        dot_nn(proj_grads[0], self_in_w[:lanes])
        + dot_nn(proj_grads[1], self_in_w[lanes : 2 * lanes])
        + dot_nn(proj_grads[2], self_in_w[2 * lanes :])
    )
    self_grads = jnp.stack(
        [trim_heads(dot_tn(grad, attn_in).astype(low)) for grad in proj_grads]
        + [trim_heads(out_weight_part.astype(low))],
    )
    _, first_back = jax.vjp(first_norm, stream, shift_vec)
    from_one, shift_own_grad = first_back(first_grad_in)
    grad_one = (grad_two + from_one).astype(low)

    self_grads, cross_parts = tie(self_grads, cross_parts)
    self_parts = scatter_rows(self_grads)
    home_grad = collect(grad_one.reshape(size, piece_len, width)).reshape(own_len, width)
    home_grad, cross_parts = tie(home_grad, cross_parts)
    cross_total = add_line(cross_parts[0], send_line(cross_parts))
    skip_bias_part = jnp.sum(home_grad.astype(f32), axis=0)
    skip_own_grad = dot_tn(home_grad, normed_own)
    skip_other_grad = dot_tn(home_grad, normed_other).astype(low)
    skip_sum = (skip_own_grad + swap_cores(skip_other_grad).astype(f32)).astype(low)
    first_sums = jnp.concatenate([down_total, up_total, cross_total], 0)
    first_sums, self_parts, skip_sum = tie(first_sums, self_parts, skip_sum)
    first_sums = share_rows(first_sums)
    self_total = add_line(self_parts[0], send_line(self_parts))
    own_in = dot_nn(home_grad, skip_own_w)
    other_in = dot_nn(home_grad, skip_other_w)
    latent_in_grad = jnp.where(core == 0, own_in, other_in)
    skip_in_grad = jnp.where(core == 0, other_in, own_in)
    latent_ln = latent_c * inverse
    skip_ln = skip_c * inverse
    skip_gain_part = jnp.concatenate(
        [jnp.sum(latent_in_grad * latent_ln, 0), jnp.sum(skip_in_grad * skip_ln, 0)]
    )
    skip_beta_part = jnp.concatenate([jnp.sum(latent_in_grad, 0), jnp.sum(skip_in_grad, 0)])
    latent_h = latent_in_grad * skip_gain_f[:width]
    skip_h = skip_in_grad * skip_gain_f[width:]
    mean_h = (jnp.sum(latent_h, -1, keepdims=True) + jnp.sum(skip_h, -1, keepdims=True)) / joined_size
    mean_hl = (
        jnp.sum(latent_h * latent_ln, -1, keepdims=True)
        + jnp.sum(skip_h * skip_ln, -1, keepdims=True)
    ) / joined_size
    latent_grad = (inverse * (latent_h - mean_h - latent_ln * mean_hl)).reshape(latent_in.shape)
    skip_grad = (inverse * (skip_h - mean_h - skip_ln * mean_hl)).reshape(latent_in.shape)

    shift_own = shift_own_grad + swap_cores(shift_own_grad)
    shift_line = rolled(
        jnp.stack([shift_own] + [from_later(shift_own, step, size) for step in range(1, size)]),
        (size - rank) % size,
    )
    line_cols = lax.dynamic_slice_in_dim(shift_line, rank * shard, shard, 1)
    condition_part = jnp.dot(line_cols, ada_weight_f.T, precision=PRECISE)

    text_half = text_size // 2
    text_rows = lax.dynamic_slice_in_dim(text_part, core * text_half, text_half, 0)
    text_away = lax.dynamic_slice_in_dim(text_part, (1 - core) * text_half, text_half, 0).astype(low)
    text_rows = (text_rows + swap_cores(text_away).astype(f32)).astype(low)
    up_bias_abs = up_bias_part.reshape(chips, size, ff_part).transpose(1, 0, 2).reshape(size, ff_half)
    up_bias_vec = jnp.stack(
        [jnp.where(core == 0, up_bias_abs, 0.0), jnp.where(core == 1, up_bias_abs, 0.0)], 1
    ).reshape(2 * size * ff_half)
    gain_rows = jnp.concatenate(
        [jnp.sum(sums[:, :2], 0)[:, :HD].reshape(2 * HD) for sums in (self_gain_sums, cross_gain_sums)]
    )
    last_row = 2 * size * ff_half % width
    vector_rows = jnp.concatenate(
        [
            skip_gain_part,
            skip_beta_part,
            skip_bias_part,
            out_bias_part,
            gain2_part,
            beta2_part,
            cross_bias_part,
            gain3_part,
            beta3_part,
            down_bias_part,
            up_bias_vec,
            gain_rows,
            jnp.zeros((width - last_row - gain_rows.shape[0],), f32),
        ]
    ).reshape(-1, width)
    first_core = core == 0
    line_rows = jnp.stack(
        [
            jnp.where(first_core, condition_part, 0.0),
            jnp.where(first_core & (rank == 0), shift_line, 0.0),
        ]
    )
    chip_rows = jnp.where(
        (jnp.arange(chips) == chip)[None, :, None, None], line_rows[:, None], 0.0
    ).reshape(2 * chips * size, width)
    time_rows = jnp.where(
        (jnp.arange(2 * chips) == 2 * chip + core)[:, None, None] & (rank == 0),
        time_emb.astype(f32)[None],
        0.0,
    ).reshape(2 * chips * sequences, width)
    vectors = jnp.concatenate([chip_rows, time_rows, vector_rows], 0)
    vector_part = 32 * -(-vectors.shape[0] // (32 * chips))
    vectors = jnp.pad(vectors, ((0, chips * vector_part - vectors.shape[0]), (0, 0)))
    vectors = vectors.astype(low).reshape(chips, vector_part, width)

    def own_cols(vector, count):
        return lax.dynamic_slice_in_dim(vector, rank * count, count, 0)

    skip_rel_grad = rolled(skip_sum.reshape(size, chips, skip_part, width), rank).transpose(1, 0, 2, 3)
    skip_rows = size * skip_part
    skip_rows_all = jnp.concatenate([skip_rel_grad.reshape(chips, skip_rows, width), vectors], 1)
    skip_rows_all, first_sums, self_total, text_rows = tie(
        skip_rows_all, first_sums, self_total, text_rows
    )
    text_pieces = []
    for turn in range(size):
        pairs = [
            (c * size + r, (r // 2) * size + (2 * (r % 2) + c + turn) % size)
            for c in range(2)
            for r in range(size)
        ]
        text_pieces.append(lax.ppermute(text_rows, ("core", "tensor"), pairs))
    text_stack = jnp.stack(text_pieces)
    text_grad = (
        jnp.stack([pick(text_stack, (rank - k) % size) for k in range(size)])
        .reshape(sequences, text_size, width)
        .astype(f32)
    )
    parts = lax.psum_scatter(
        skip_rows_all.reshape(-1, width), "chip", scatter_dimension=0, tiled=True
    )
    self_total, parts = tie(self_total, parts)
    self_sum = share_rows(self_total)
    vector_mine = parts[skip_rows:]
    skip_total = parts[:skip_part].astype(f32)
    vector_line = [vector_mine]
    for step in range(1, size):
        arrived = from_earlier(
            jnp.concatenate([parts[step * skip_part : (step + 1) * skip_part], vector_mine], 0), step, size
        )
        skip_total = skip_total + arrived[:skip_part].astype(f32)
        vector_line.append(arrived[skip_part:])
    vector_line = jnp.stack(vector_line)
    vector_total = pick(vector_line, rank).astype(f32)
    for source in range(1, size):
        vector_total = vector_total + pick(vector_line, (rank - source) % size).astype(f32)
    skip_send = jnp.concatenate([skip_total, vector_total], 0).astype(low)
    skip_send, self_sum = tie(skip_send, self_sum)
    total = share_rows(skip_send).reshape(chips, skip_part + vector_part, width)
    first_sums = first_sums.reshape(chips, 2 * ff_part + half, width)
    down_sum = first_sums[:, :ff_part].reshape(ff_half, width)
    up_sum = first_sums[:, ff_part : 2 * ff_part].reshape(ff_half, width)
    cross_sum = first_sums[:, 2 * ff_part :]
    down0, down1 = by_core(down_sum)
    down_weight_grad = jnp.concatenate([down0, down1], 0).astype(f32)
    up0, up1 = by_core(up_sum)
    up_weight_grad = jnp.concatenate([up0.T, up1.T], 1).astype(f32)
    cross0, cross1 = (part.reshape(4, half, width) for part in by_core(cross_sum))

    def cols_of(first, second):
        return jnp.concatenate([first.T, second.T], 1).astype(f32)

    def rows_of(first, second):
        return jnp.concatenate([first, second], 0).astype(f32)

    cross_query_weight_grad = cols_of(cross0[0], cross1[0])
    cross_kv_weight_grad = jnp.stack([cols_of(cross0[i], cross1[i]) for i in (1, 2)])
    cross_out_weight_grad = rows_of(cross0[3], cross1[3])
    self0, self1 = (part.reshape(4, half, width) for part in by_core(self_sum))
    qkv_weight_grad = jnp.stack([cols_of(self0[i], self1[i]) for i in range(3)])
    out_weight_grad = rows_of(self0[3], self1[3])
    total_other = swap_cores(total)
    skip0 = jnp.where(core == 0, total[:, :skip_part], total_other[:, :skip_part])
    skip1 = jnp.where(core == 0, total_other[:, :skip_part], total[:, :skip_part])
    skip_weight_grad = jnp.concatenate(
        [skip0.reshape(shard, width).T, skip1.reshape(shard, width).T], 0
    ).astype(f32)
    summed = (total[:, skip_part:].astype(f32) + total_other[:, skip_part:].astype(f32)).reshape(-1, width)
    seqs = chips * size
    own_seq = (chip * 2 + core) * sequences
    time_back = lax.dynamic_slice_in_dim(summed[:seqs], own_seq, sequences, 0)
    _, silu_back = jax.vjp(jax.nn.silu, time_emb.astype(f32))
    time_grad = silu_back(time_back)[0]
    shift_cols = lax.dynamic_slice_in_dim(summed[seqs : 2 * seqs], rank * shard, shard, 1)
    condition_all = jax.nn.silu(summed[2 * seqs : 3 * seqs])
    ada_bias_grad = jnp.sum(shift_cols, axis=0)
    ada_weight_grad = jnp.dot(condition_all.T, shift_cols, precision=PRECISE)
    flat = summed[3 * seqs :].reshape(-1)
    rows_at = [flat[width * i : width * (i + 1)] for i in range(12)]
    up_bias_sum = flat[12 * width : 12 * width + 2 * size * ff_half]
    gain_sums = flat[12 * width + 2 * size * ff_half :][: 4 * HD].reshape(2, 2, HD)
    return (
        output_home,
        stats_home,
        latent_grad,
        skip_grad,
        text_grad,
        time_grad,
        flat[: 2 * width],
        flat[2 * width : 4 * width],
        skip_weight_grad,
        own_cols(rows_at[4], shard),
        ada_weight_grad,
        ada_bias_grad,
        qkv_weight_grad,
        gain_sums[0],
        out_weight_grad,
        rows_at[5],
        rows_at[6],
        rows_at[7],
        cross_query_weight_grad,
        cross_kv_weight_grad,
        gain_sums[1],
        cross_out_weight_grad,
        rows_at[8],
        rows_at[9],
        rows_at[10],
        up_weight_grad,
        own_cols(up_bias_sum, 2 * ff_half),
        down_weight_grad,
        rows_at[11],
    )


def specs(dp):
    in_specs = (
        P(dp, "tensor", None),
        P(dp, "tensor", None),
        P(dp, None, None),
        P(dp),
        P(dp, None),
        P(dp, None, None),
        P(),
        P(),
        P(None, "tensor"),
        P("tensor"),
        P(None, "tensor"),
        P("tensor"),
        P(None, None, "tensor"),
        P(),
        P("tensor", None),
        P(),
        P(),
        P(),
        P(None, "tensor"),
        P(None, None, "tensor"),
        P(),
        P("tensor", None),
        P(),
        P(),
        P(),
        P(None, "tensor"),
        P("tensor"),
        P("tensor", None),
        P(),
        P(dp, "tensor", None),
    )
    out_specs = (
        P(dp, "tensor", None),
        P(dp, None, "tensor"),
        P(dp, "tensor", None),
        P(dp, "tensor", None),
        P(dp, None, None),
        P(dp, None),
        P(),
        P(),
        P(None, "tensor"),
        P("tensor"),
        P(None, "tensor"),
        P("tensor"),
        P(None, None, "tensor"),
        P(),
        P("tensor", None),
        P(),
        P(),
        P(),
        P(None, "tensor"),
        P(None, None, "tensor"),
        P(),
        P("tensor", None),
        P(),
        P(),
        P(),
        P(None, "tensor"),
        P("tensor"),
        P("tensor", None),
        P(),
    )
    return in_specs, out_specs


def solution(mesh):
    dp_size, size = mesh.shape["dp"], mesh.shape["tensor"]
    if dp_size == 8 and size == 4:
        grid = Mesh(mesh.devices.reshape(dp_size // 2, 2, size), ("chip", "core", "tensor"))
        in_specs, out_specs = specs(("chip", "core"))
        return jax.shard_map(
            chip_local, mesh=grid, in_specs=in_specs, out_specs=out_specs, check_vma=False
        )
    in_specs, out_specs = specs("dp")
    return jax.shard_map(
        tensor_local, mesh=mesh, in_specs=in_specs, out_specs=out_specs, check_vma=False
    )
```
